32 devices in a mesh: area: 8 (over z, x), row: 4 (over y, core).
Axes of the slice: x: 2, y: 2, z: 4, core: 2. Of those that a mesh axis runs over, the one named last changes fastest.
Arguments:
- conductance_inverse: float32 [32, 1024, 1024], P(('area', 'row')), as said below
- cap_history: float32 [32, 1024, 128], P(('area', 'row')), may hold values from -3 to 3
- cap_conductance: float32 [32, 1024], P(('area', 'row')), may hold values from 0.5 to 0.8
- wave_history: float32 [32, 40, 32, 128], P(('area', 'row')), may hold values from -6 to 6
- line_partner: int32 [32, 32], P(('area', 'row')), may hold values from 0 to 31, as said below
- line_node: int32 [32, 32], P(('area', 'row')), may hold values from 0 to 1023
- line_delay: int32 [32, 32], P(('area', 'row')), may hold values from 20 to 40
- line_admittance: float32 [32, 32], P(('area', 'row')), may hold values from 0.2 to 1
- conv_node: int32 [32, 64], P(('area', 'row')), may hold values from 0 to 1023
- conv_count: int32 [32], P(('area', 'row')), may hold values from 1 to 64, as said below
- conv_state: float32 [32, 2, 64, 128], P(('area', 'row')), may hold values from -3 to 3
- conv_reference: float32 [32, 2, 64, 128], P(('area', 'row')), may hold values from -4 to 4
- conv_rate: float32 [32, 64], P(('area', 'row')), may hold values from 0.03 to 0.6
- conv_limit: float32 [32, 64], P(('area', 'row')), may hold values from 1 to 2.5
- port_node: int32 [32, 8], P(('area', 'row')), may hold values from 0 to 1023
- port_admittance: float32 [32, 8], P(('area', 'row')), may hold values from 0.3 to 1.2
- port_voltage_prev: float32 [2, 32, 8, 128], P(None, ('area', 'row')), may hold values from -5 to 5
- port_bus: int32 [32, 8], P('area'), may hold values from 0 to 20479
- transfer_impedance: float32 [2, 20480, 256], P(None, 'row', 'area'), may hold values from -0.75 to 0.75
Outputs:
- waves: float32 [32, 20, 32, 128], P(('area', 'row'))
- cap_history_out: float32 [32, 1024, 128], P(('area', 'row'))
- conv_state_out: float32 [32, 2, 64, 128], P(('area', 'row'))
- bus_voltage: float32 [2, 20480, 128], P(None, 'row')
- port_voltage: float32 [2, 32, 8, 128], P(None, ('area', 'row'))
The draws below stay inside these ranges and needn't reach their ends.
Inputs may be any that keep to these rules, and one draw needn't show every extreme that they name: Slot l < 16 of subnetwork s and slot l + 16 of subnetwork (s + k_l) mod 32 are the two ends of one line, with k_l in 1 or 2 the same for every subnetwork and exactly 12 of the k_l equal to 1; so line_partner[s, l] = (s + k_l) mod 32 and line_partner[s, l + 16] = (s - k_l) mod 32. `conv_count`: some subnetwork has all 64 converters in service. `conductance_inverse`: each subnetwork's inverse nodal conductance matrix.
All inputs are finite; a program needn't handle non-finite values.
Results may differ from the reference program's by a relative error of at most 0.0003.
Values sent between devices are 32-bit elements; how exact they have to be, the bound alone decides.
A program may use at most 64 MiB of HBM per device.

```python
import math
import jax
import jax.numpy as jnp
from jax import lax

NODES = 1024
CASES = 128
STEPS = 20
HIST = 40
LINES = 32
NEAR = 12
CONV = 64
PORTS = 8
NB = 20480
SUBNETS = 32
NPORT = 256


def draw_conductance_inverse(key, part):
    first, second = jax.random.split(key)
    diagonal = 0.5 + 0.4 * jax.random.uniform(first, (SUBNETS, NODES), dtype=jnp.float32)
    spread = jax.random.normal(second, (SUBNETS, NODES, NODES), dtype=jnp.float32) * (0.2 / NODES ** 0.5)
    return spread + diagonal[:, :, None] * jnp.eye(NODES, dtype=jnp.float32)[None, :, :]


def draw_line_partner(key, part):
    order = jax.random.permutation(jax.random.fold_in(key, 11), LINES // 2)
    reach = jnp.where(order < NEAR, 1, 2).astype(jnp.int32)
    subnet = jnp.arange(SUBNETS, dtype=jnp.int32)[:, None]
    upper = (subnet + reach[None, :]) % SUBNETS
    lower = (subnet - reach[None, :]) % SUBNETS
    return jnp.concatenate([upper, lower], axis=1).astype(jnp.int32)


def draw_conv_count(key, part):
    first, second = jax.random.split(jax.random.fold_in(key, 23))
    counts = jax.random.randint(first, (SUBNETS,), 1, CONV + 1, dtype=jnp.int32)
    where_full = jax.random.randint(second, (), 0, SUBNETS, dtype=jnp.int32)
    return counts.at[where_full].set(CONV).astype(jnp.int32)


def place_ends(result, rng, least, top_value):
    extent = result.shape
    place = [jax.random.randint(jax.random.fold_in(rng, axis), (), 0, extent[axis]) for axis in range(len(extent))]
    result = result.at[tuple(place)].set(least)
    longest = extent.index(max(extent))
    place[longest] = (place[longest] + 1) % extent[longest]
    return result.at[tuple(place)].set(top_value)


def block_levels(key, extent, pieces, low, top_value):
    def one(dim, parts):
        steps = jax.random.uniform(jax.random.fold_in(jax.random.fold_in(key, 6), dim), (parts,), jnp.float32, low / len(pieces), top_value / len(pieces))
        return jnp.repeat(jnp.exp(steps), extent[dim] // parts).reshape((-1,) + (1,) * (len(extent) - dim - 1))

    gain = one(*pieces[0])
    for cut in pieces[1:]:
        gain = gain * one(*cut)
    return gain


def noise(rng, extent, deviation, most, cuts=(), held_as=jnp.bfloat16):
    values = jax.random.normal(rng, extent, jnp.float32) * deviation
    if len(cuts) > 0:
        values = block_levels(rng, extent, cuts, -0.22, 0.18) * values
    return jnp.clip(values, min=-most, max=most).astype(held_as)


def setup_inputs(seed: int = 0) -> dict:
    streams_of = jax.random.split(jax.random.key(seed), 20)
    return {
        "conductance_inverse": draw_conductance_inverse(jax.random.fold_in(streams_of[19], 71), 0),
        "cap_history": noise(streams_of[1], (SUBNETS, NODES, CASES), 0.5, 3.0, ((0, 32),), jnp.float32),
        "cap_conductance": jnp.clip(0.5 + 0.3 * jax.random.uniform(streams_of[2], (SUBNETS, NODES), jnp.float32) ** block_levels(streams_of[2], (SUBNETS, NODES), ((0, 32),), -0.2, 0.2), 0.5, 0.8),
        "wave_history": noise(streams_of[3], (SUBNETS, HIST, LINES, CASES), 1.0, 6.0, ((0, 32),), jnp.float32),
        "line_partner": draw_line_partner(jax.random.fold_in(streams_of[19], 71), 0),
        "line_node": place_ends(jax.random.randint(streams_of[5], (SUBNETS, LINES), 0, NODES), jax.random.fold_in(streams_of[5], 1), 0, NODES - 1).astype(jnp.int32),
        "line_delay": place_ends(jax.random.randint(streams_of[6], (SUBNETS, LINES), STEPS, 2 * STEPS + 1), jax.random.fold_in(streams_of[6], 1), STEPS, 2 * STEPS).astype(jnp.int32),
        "line_admittance": jnp.clip(0.2 + 0.8 * jax.random.uniform(streams_of[7], (SUBNETS, LINES), jnp.float32) ** block_levels(streams_of[7], (SUBNETS, LINES), ((0, 32),), -0.2, 0.2), 0.2, 1.0),
        "conv_node": place_ends(jax.random.randint(streams_of[8], (SUBNETS, CONV), 0, NODES), jax.random.fold_in(streams_of[8], 1), 0, NODES - 1).astype(jnp.int32),
        "conv_count": draw_conv_count(jax.random.fold_in(streams_of[19], 71), 0),
        "conv_state": noise(streams_of[10], (SUBNETS, 2, CONV, CASES), 0.5, 3.0, ((0, 32),), jnp.float32),
        "conv_reference": noise(streams_of[11], (SUBNETS, 2, CONV, CASES), 1.0, 4.0, ((0, 32),), jnp.float32),
        "conv_rate": jnp.clip(jnp.exp(math.log(0.6) - 2.9957323 * jax.random.uniform(streams_of[12], (SUBNETS, CONV), jnp.float32) ** block_levels(streams_of[12], (SUBNETS, CONV), ((0, 32),), -0.2, 0.2)), 0.03, 0.6),
        "conv_limit": jnp.clip(1.0 + 1.5 * jax.random.uniform(streams_of[13], (SUBNETS, CONV), jnp.float32) ** block_levels(streams_of[13], (SUBNETS, CONV), ((0, 32),), -0.2, 0.2), 1.0, 2.5),
        "port_node": place_ends(jax.random.randint(streams_of[14], (SUBNETS, PORTS), 0, NODES), jax.random.fold_in(streams_of[14], 1), 0, NODES - 1).astype(jnp.int32),
        "port_admittance": jnp.clip(0.3 + 0.90000004 * jax.random.uniform(streams_of[15], (SUBNETS, PORTS), jnp.float32) ** block_levels(streams_of[15], (SUBNETS, PORTS), ((0, 32),), -0.2, 0.2), 0.3, 1.2),
        "port_voltage_prev": noise(streams_of[16], (2, SUBNETS, PORTS, CASES), 1.0, 5.0, ((1, 32),), jnp.float32),
        "port_bus": place_ends(jax.random.randint(streams_of[17], (SUBNETS, PORTS), 0, NB), jax.random.fold_in(streams_of[17], 1), 0, NB - 1).astype(jnp.int32),
        "transfer_impedance": noise(streams_of[18], (2, NB, NPORT), (NPORT // 4) ** -0.5, 0.75, ((1, 4), (2, 8)), jnp.float32),
    }


HIGHEST = lax.Precision.HIGHEST
SAG_FACTOR = 0.3


def window(ginv, start_hist, gcap, incoming, lnode, ladm, cnode, ccount, cstate, setpoint_flow, crate, climit, pnode, padm, pvolt):
    nodes = ginv.shape[0]
    lines = lnode.shape[0]
    convs = cnode.shape[0]
    index = jnp.concatenate([lnode, cnode, pnode]).astype(jnp.int32)
    onehot = (jnp.arange(nodes, dtype=jnp.int32)[:, None] == index[None, :]).astype(jnp.float32)
    picker = onehot.T
    live = (jnp.arange(convs, dtype=jnp.int32) < ccount)[:, None]
    angles = jnp.arange(1, STEPS + 1, dtype=jnp.float32) * jnp.float32(2.0 * math.pi / STEPS)
    limit = climit[:, None]
    slew_limit = crate[:, None]

    def advance(carry, inputs):
        hist_now, inverter_axial_part, inverter_normal_part, acc_re, acc_im = carry
        inward, angle = inputs
        angle_cos_factor = jnp.cos(angle)
        angle_sin_factor = jnp.sin(angle)
        drive = jnp.where(live, inverter_axial_part * angle_cos_factor - inverter_normal_part * angle_sin_factor, 0.0)
        source = padm[:, None] * (pvolt[0] * angle_cos_factor - pvolt[1] * angle_sin_factor)
        stacked = jnp.concatenate([inward, drive, source], axis=0)
        right = hist_now + jnp.dot(onehot, stacked, precision=HIGHEST)
        volt = jnp.dot(ginv, right, precision=HIGHEST)
        probe = jnp.dot(picker, volt, precision=HIGHEST)
        at_line = probe[:lines]
        inverter_emf = probe[lines:lines + convs]
        at_port = probe[lines + convs:]
        outward = 2.0 * ladm[:, None] * at_line - inward
        flow = source - padm[:, None] * at_port
        acc_re = acc_re + flow * angle_cos_factor
        acc_im = acc_im - flow * angle_sin_factor
        unclipped_axial_part = inverter_axial_part + slew_limit * (setpoint_flow[0] - inverter_axial_part) - SAG_FACTOR * inverter_emf * angle_cos_factor
        unclipped_normal_part = inverter_normal_part + slew_limit * (setpoint_flow[1] - inverter_normal_part) + SAG_FACTOR * inverter_emf * angle_sin_factor
        inverter_axial_part = jnp.where(live, limit * jnp.tanh(unclipped_axial_part / limit), inverter_axial_part)
        inverter_normal_part = jnp.where(live, limit * jnp.tanh(unclipped_normal_part / limit), inverter_normal_part)
        hist_now = 2.0 * gcap[:, None] * volt - hist_now
        return (hist_now, inverter_axial_part, inverter_normal_part, acc_re, acc_im), outward

    zeros = jnp.zeros(pvolt.shape[1:], dtype=jnp.float32)
    carry = (start_hist, cstate[0], cstate[1], zeros, zeros)
    carry, outward = lax.scan(advance, carry, (incoming, angles))
    hist_end, inverter_axial_part, inverter_normal_part, acc_re, acc_im = carry
    current = jnp.stack([acc_re, acc_im]) * jnp.float32(2.0 / STEPS)
    return outward, hist_end, jnp.stack([inverter_axial_part, inverter_normal_part]), current


def reference(conductance_inverse, cap_history, cap_conductance, wave_history, line_partner, line_node, line_delay, line_admittance, conv_node, conv_count, conv_state, conv_reference, conv_rate, conv_limit, port_node, port_admittance, port_voltage_prev, port_bus, transfer_impedance):
    remote = (jnp.arange(LINES, dtype=jnp.int32) + LINES // 2) % LINES
    times = jnp.arange(STEPS, dtype=jnp.int32)

    def one_subnet(items):
        ginv, start_hist, gcap, partner, lnode, delay, ladm, cnode, ccount, cstate, setpoint_flow, crate, climit, pnode, padm, pvolt = items
        rows = wave_history[partner, :, remote, :]
        where_now = (times[None, :] - delay[:, None] + HIST).astype(jnp.int32)
        delayed = jnp.take_along_axis(rows, where_now[:, :, None], axis=1)
        incoming = jnp.transpose(delayed, (1, 0, 2))
        return window(ginv, start_hist, gcap, incoming, lnode, ladm, cnode, ccount, cstate, setpoint_flow, crate, climit, pnode, padm, pvolt)

    pvolt_all = jnp.transpose(port_voltage_prev, (1, 0, 2, 3))
    waves, hist_end, conv_out, current = lax.map(one_subnet, (conductance_inverse, cap_history, cap_conductance, line_partner, line_node, line_delay, line_admittance, conv_node, conv_count, conv_state, conv_reference, conv_rate, conv_limit, port_node, port_admittance, pvolt_all))
    flat = jnp.transpose(current, (1, 0, 2, 3)).reshape(2, SUBNETS * PORTS, CASES)
    real = jnp.dot(transfer_impedance[0], flat[0], precision=HIGHEST) - jnp.dot(transfer_impedance[1], flat[1], precision=HIGHEST)
    imag = jnp.dot(transfer_impedance[0], flat[1], precision=HIGHEST) + jnp.dot(transfer_impedance[1], flat[0], precision=HIGHEST)
    bus_voltage = jnp.stack([real, imag])
    port_voltage = bus_voltage[:, port_bus.reshape(-1).astype(jnp.int32), :].reshape(2, SUBNETS, PORTS, CASES)
    return waves, hist_end, conv_out, bus_voltage, port_voltage
```

```python
import functools
import math

import jax
import jax.numpy as jnp
from jax import lax
from jax.experimental import pallas as pl
from jax.experimental.pallas import tpu as pltpu
from jax.sharding import PartitionSpec as P

STEPS = 20
HIST = 40
SAG_FACTOR = 0.3
F32 = jnp.float32
BF16 = jnp.bfloat16
MESH = pl.DeviceIdType.MESH
SUBS = 10


def shifted(x, by):
    axes = ("area", "row")
    size = lax.axis_size(axes)
    return lax.ppermute(x, axes, [(i, (i + by) % size) for i in range(size)])


def split(x):
    high = x.astype(BF16)
    return high, (x - high.astype(F32)).astype(BF16)


def mm(a, b):
    return lax.dot_general(a, b, (((1,), (0,)), ((), ())), preferred_element_type=F32)


def columns(row, count):
    return jnp.broadcast_to(row, (128, count)).T


def window_kernel(
    lines,
    convs,
    ports,
    reach_ref,
    delay_ref,
    trig_ref,
    count_ref,
    index_ref,
    coef_ref,
    ginv_ref,
    gcap_ref,
    hist_ref,
    below1_ref,
    below2_ref,
    above1_ref,
    above2_ref,
    state_ref,
    target_ref,
    pvolt_ref,
    port_bus_ref,
    zc_ref,
    waves_ref,
    hist_out_ref,
    state_out_ref,
    port_ref,
    bus_ref,
    big,
    wj,
    wx,
    cap2,
    xs,
    current_ref,
    zin,
    cin,
    vbus,
    flat_ref,
    rh,
    rl,
    zs,
    zr,
    zf,
    rs,
    rr,
    cs,
    cr,
    zlocal,
    os,
    orr,
    fs,
    xf,
    xr,
    olocal,
    picked,
    landed,
    ps,
    pr,
):
    nodes = ginv_ref.shape[0]
    probes = 128
    half = lines // 2
    rows = 256
    areas, group = cin.shape[0], cin.shape[1]
    pieces, depth, width = zin.shape[0], zin.shape[2], zin.shape[3]
    inner = 2 ** ((areas.bit_length() - 1) // 2)
    outer = areas // inner
    span_rows = bus_ref.shape[1] // outer
    chunk = span_rows // inner
    a = lax.axis_index("area")
    r = lax.axis_index("row")
    zi = lax.div(a, inner)
    xi = lax.rem(a, inner)

    barrier = pltpu.get_barrier_semaphore()
    for d in range(1, areas):
        pl.semaphore_signal(barrier, inc=1, device_id=(lax.rem(a + d, areas), r), device_id_type=MESH)
    for d in range(1, group):
        pl.semaphore_signal(barrier, inc=1, device_id=(a, lax.rem(r + d, group)), device_id_type=MESH)
    pl.semaphore_wait(barrier, areas + group - 2)

    def send(src, dst, ssem, rsem, to):
        return pltpu.make_async_remote_copy(
            src_ref=src, dst_ref=dst, send_sem=ssem, recv_sem=rsem, device_id=to, device_id_type=MESH
        )

    def mate(e):
        return zi * inner + lax.rem(xi + e, inner)

    def part_of(plane, p):
        return zc_ref.at[:, pl.ds(pl.multiple_of((plane * pieces + p) * width, 128), width)]

    z_sends = []
    own_z = []
    for p in range(pieces):
        copy = pltpu.make_async_copy(part_of(zi, p), zin.at[p, a], zlocal.at[p])
        copy.start()
        own_z.append(copy)
        for d in range(1, outer):
            plane = lax.rem(zi + d, outer)
            copy = send(part_of(plane, p), zin.at[p, a], zs.at[p, d], zr.at[p, a], (plane * inner + xi, r))
            copy.start()
            z_sends.append(copy)
        for e in range(1, inner):
            copy = send(part_of(zi, p), zin.at[p, a], zf.at[p, 0, e], zr.at[p, a], (mate(e), r))
            copy.start()
            z_sends.append(copy)

    def relay_z(p):
        for d in range(1, outer):
            owner = lax.rem(zi + outer - d, outer) * inner + xi
            block = zin.at[p, owner]
            send(block, block, zs.at[p, d], zr.at[p, owner], (owner, r)).wait_recv()
            for e in range(1, inner):
                copy = send(block, block, zf.at[p, d, e], zr.at[p, owner], (mate(e), r))
                copy.start()
                z_sends.append(copy)

    index = columns(index_ref[...].astype(F32), probes).astype(jnp.int32)
    for c in range(nodes // 128):
        lane = lax.broadcasted_iota(jnp.int32, (probes, 128), 1) + 128 * c
        cap2[:, c * 128 : (c + 1) * 128] = jnp.where(index == lane, 1.0, 0.0)
    pick = cap2[...].astype(BF16)
    scatter = cap2[...].T.astype(BF16)
    for b in range(nodes // rows):
        span = pl.ds(b * rows, rows)
        high, low = split(ginv_ref[span, :])
        big[span, 0:nodes] = high
        big[span, nodes : 2 * nodes] = low
    tail = pl.ds(nodes, probes)
    big[tail, :nodes] = mm(pick, big[0:nodes, 0:nodes]).astype(BF16)
    big[tail, nodes : 2 * nodes] = mm(pick, big[0:nodes, nodes : 2 * nodes]).astype(BF16)
    big[:, 2 * nodes : 2 * nodes + 128] = mm(big[:, 0:nodes], scatter).astype(BF16)
    big[:, 2 * nodes + 128 :] = mm(big[:, nodes : 2 * nodes], scatter).astype(BF16)
    gcap = 2.0 * columns(gcap_ref[...], nodes)

    def put_state(value):
        high, low = split(value)
        wj[:, 0:128] = high
        wj[:, 128:256] = low

    hist_out_ref[...] = hist_ref[...]
    put_state(hist_ref[...])
    state_out_ref[...] = state_ref[...]
    current_ref[...] = jnp.zeros_like(current_ref)
    coef = coef_ref[...]
    two_adm = columns(coef[0:1], 128)[0:lines]
    rate = columns(coef[1:2], 128)[lines : lines + convs]
    limit = columns(coef[2:3], 128)[lines : lines + convs]
    padm = columns(coef[0:1], 128)[lines + convs : lines + convs + ports]
    live = lax.broadcasted_iota(jnp.int32, (convs, 128), 0) < count_ref[0]
    xs[lines + convs + ports :, :] = jnp.zeros((probes - lines - convs - ports, 128), F32)

    def step(t, carry):
        cosine = trig_ref[0, t]
        sine = trig_ref[1, t]
        for l in range(half):
            up = jnp.clip(t - delay_ref[l] + HIST, 0, HIST - 1)
            down = jnp.clip(t - delay_ref[l + half] + HIST, 0, HIST - 1)
            near = reach_ref[l] == 1
            xs[l : l + 1, :] = jnp.where(near, above1_ref[up, l : l + 1, :], above2_ref[up, l : l + 1, :])
            xs[l + half : l + half + 1, :] = jnp.where(
                near, below1_ref[down, l : l + 1, :], below2_ref[down, l : l + 1, :]
            )
        inward = xs[0:lines, :]
        axial = state_out_ref[0]
        normal = state_out_ref[1]
        source = padm * (pvolt_ref[0] * cosine - pvolt_ref[1] * sine)
        xs[lines : lines + convs, :] = jnp.where(live, axial * cosine - normal * sine, 0.0)
        xs[lines + convs : lines + convs + ports, :] = source
        high, low = split(xs[...])
        wx[0:128, 0:128] = high
        wx[128:256, 0:128] = high
        wx[0:128, 128:256] = low
        wx[128:256, 128:256] = low

        def apply(start, size):
            span = pl.ds(start, size)
            both = (
                mm(big[span, 0:nodes], wj[...])
                + mm(big[span, nodes : 2 * nodes], wj[...])
                + mm(big[span, 2 * nodes :], wx[...])
            )
            return both[:, 0:128] + both[:, 128:256]

        probe = apply(nodes, probes)
        volts = apply(0, nodes)
        waves_ref[t] = two_adm * probe[0:lines] - inward
        emf = probe[lines : lines + convs]
        flow = source - padm * probe[lines + convs : lines + convs + ports]
        current_ref[0] += flow * cosine
        current_ref[1] -= flow * sine
        new_axial = axial + rate * (target_ref[0] - axial) - SAG_FACTOR * emf * cosine
        new_normal = normal + rate * (target_ref[1] - normal) + SAG_FACTOR * emf * sine
        state_out_ref[0] = jnp.where(live, limit * jnp.tanh(new_axial / limit), axial)
        state_out_ref[1] = jnp.where(live, limit * jnp.tanh(new_normal / limit), normal)
        after = gcap * volts - hist_out_ref[...]
        hist_out_ref[...] = after
        put_state(after)
        return carry

    stops = [STEPS * 9 // 10 - (pieces - 1 - p) * STEPS * 2 // 5 for p in range(pieces)]
    at = 0
    for p, stop in enumerate(stops):
        lax.fori_loop(at, stop, step, 0)
        relay_z(p)
        at = stop
    lax.fori_loop(at, STEPS, step, 0)
    cin[a, r] = current_ref[...] * (2.0 / STEPS)

    copies = []
    for d in range(1, group):
        block = cin.at[a, r]
        copy = send(block, block, rs.at[d], rr.at[d], (a, lax.rem(r + d, group)))
        copy.start()
        copies.append(copy)
    for copy in copies:
        copy.wait()
    copies = []
    for d in range(1, areas):
        block = cin.at[a]
        copy = send(block, block, cs.at[d], cr.at[d], (lax.rem(a + d, areas), r))
        copy.start()
        copies.append(copy)
    for copy in copies:
        copy.wait()
    members = group * ports
    for i in range(areas):
        for j in range(group):
            re, im = cin[i, j, 0], cin[i, j, 1]
            top = i * depth + j * ports
            flat_ref[top : top + ports, 0:128] = re
            flat_ref[top : top + ports, 128:256] = im
            flat_ref[top + members : top + members + ports, 0:128] = -im
            flat_ref[top + members : top + members + ports, 128:256] = re
    high, low = split(flat_ref[...])
    rh[...] = high
    rl[...] = low

    for p in range(pieces):
        own_z[p].wait()
    for copy in z_sends:
        copy.wait_send()
    for p in range(pieces):
        for e in range(1, inner):
            for q in range(outer):
                owner = q * inner + lax.rem(xi + e, inner)
                block = zin.at[p, owner]
                send(block, block, zf.at[p, 0, e], zr.at[p, owner], (owner, r)).wait_recv()

    def product(p):
        high, low = split(zin[p].reshape(areas * depth, width).T)
        total = mm(high, rh[...]) + mm(low, rh[...]) + mm(high, rl[...])
        keep = min(width, span_rows)
        rows = pl.ds(pl.multiple_of(zi * span_rows + p * width, 8), keep)
        vbus[0, rows, :] = total[:keep, 0:128]
        vbus[1, rows, :] = total[:keep, 128:256]

    cuts = SUBS
    sub = chunk // cuts

    def region(plane, x, k):
        top = pl.multiple_of(plane * span_rows + x * chunk + k * sub, 8)
        return vbus.at[:, pl.ds(top, sub), :]

    def emit(plane, x, count, sem):
        rows = pl.ds(pl.multiple_of(plane * span_rows + x * chunk, 8), count)
        return pltpu.make_async_copy(vbus.at[:, rows, :], bus_ref.at[:, rows, :], sem)

    def plane_at(plane):
        return (plane * inner + xi, r)

    can_up = zi + 1 < outer
    can_down = zi >= 1

    def launch(k):
        up = send(region(zi, xi, k), region(zi, xi, k), os.at[0, k], orr.at[zi, k], plane_at(zi + 1))
        down = send(region(zi, xi, k), region(zi, xi, k), os.at[1, k], orr.at[zi, k], plane_at(zi - 1))
        return up, down

    if pieces == inner:
        product(xi)
    else:
        for p in range(pieces):
            product(p)
    for k in range(cuts):
        up, down = launch(k)
        pl.when(can_up)(up.start)
        pl.when(can_down)(down.start)
    if pieces == inner:
        for i in range(1, pieces):
            product(lax.rem(xi + i, inner))
    local = emit(zi, 0, span_rows, olocal.at[0, 0, 0])
    local.start()

    def hops(d):
        return ((zi - d, zi - d >= 0, zi + 1, can_up), (zi + d, zi + d < outer, zi - 1, can_down))

    def relay(plane, k, d, side, ahead):
        block = region(plane, xi, k)
        onward = send(block, block, fs.at[side, d, k], orr.at[plane, k], plane_at(ahead))
        across = [
            send(block, block, xf.at[side, d, e, k], xr.at[plane, xi, k], (mate(e), r)) for e in range(1, inner)
        ]
        return onward, across

    for d in range(1, outer):
        for k in range(cuts):
            for side, (plane, have, ahead, go) in enumerate(hops(d)):

                @pl.when(have)
                def _(plane=plane, k=k, d=d, side=side, ahead=ahead, go=go):
                    onward, across = relay(plane, k, d, side, ahead)
                    onward.wait_recv()
                    pl.when(go)(onward.start)
                    for copy in across:
                        copy.start()

    for d in range(1, outer):
        for side, (plane, have, ahead, go) in enumerate(hops(d)):

            @pl.when(have)
            def _(plane=plane, d=d, side=side):
                emit(plane, xi, chunk, olocal.at[side, d, 0]).start()
                for e in range(1, inner):
                    x = lax.rem(xi + e, inner)
                    for k in range(cuts):
                        block = region(plane, x, k)
                        send(block, block, xf.at[side, d, e, k], xr.at[plane, x, k], (mate(e), r)).wait_recv()
                    emit(plane, x, chunk, olocal.at[side, d, e]).start()

    members = port_bus_ref.shape[0] // group
    for j in range(group):
        for p in range(members):
            place = port_bus_ref[j * members + p] - r * bus_ref.shape[1]
            inside = (place >= 0) & (place < bus_ref.shape[1])
            place = jnp.clip(place, 0, bus_ref.shape[1] - 1)
            for part in range(2):
                value = vbus[part, pl.ds(place, 1), :]
                picked[j, part, p : p + 1, :] = jnp.where(inside, value, 0.0)

    def hand(d):
        to = lax.rem(r + d, group)
        return send(picked.at[to], landed.at[r], ps.at[d], pr.at[d], (a, to))

    for d in range(1, group):
        hand(d).start()
    for d in range(1, outer):
        for side, (plane, have, ahead, go) in enumerate(hops(d)):

            @pl.when(have)
            def _(plane=plane, d=d, side=side, ahead=ahead, go=go):
                for k in range(cuts):
                    onward, across = relay(plane, k, d, side, ahead)
                    pl.when(go)(onward.wait_send)
                    for copy in across:
                        copy.wait_send()
                for e in range(inner):
                    emit(plane, lax.rem(xi + e, inner), chunk, olocal.at[side, d, e]).wait()

    for k in range(cuts):
        up, down = launch(k)
        pl.when(can_up)(up.wait_send)
        pl.when(can_down)(down.wait_send)
    for d in range(1, group):
        hand(d).wait()
    value = picked[r]
    for d in range(1, group):
        value = value + landed[lax.rem(r + d, group)]
    port_ref[...] = value
    local.wait()


def vmem():
    return pl.BlockSpec(memory_space=pltpu.VMEM)


def smem():
    return pl.BlockSpec(memory_space=pltpu.SMEM)


def per_device(
    conductance_inverse,
    cap_history,
    cap_conductance,
    wave_history,
    line_partner,
    line_node,
    line_delay,
    line_admittance,
    conv_node,
    conv_count,
    conv_state,
    conv_reference,
    conv_rate,
    conv_limit,
    port_node,
    port_admittance,
    port_voltage_prev,
    port_bus,
    transfer_impedance,
):
    subnets = lax.axis_size(("area", "row"))
    own = lax.axis_index(("area", "row"))
    history = wave_history[0]
    lines = history.shape[1]
    half = lines // 2
    cases = history.shape[2]
    nodes = conductance_inverse.shape[1]
    convs = conv_node.shape[1]
    ports = port_node.shape[1]
    upper = history[:, :half]
    lower = history[:, half:]
    below1 = shifted(upper, 1)
    above1 = shifted(lower, -1)
    below2 = shifted(upper, 2)
    above2 = shifted(lower, -2)
    reach = (line_partner[0] - own) % subnets
    areas = lax.axis_size("area")
    group = lax.axis_size("row")
    bus_rows = transfer_impedance.shape[1]
    members = transfer_impedance.shape[2]
    inner = 2 ** ((areas.bit_length() - 1) // 2)
    outer = areas // inner
    span_rows = bus_rows // outer
    padded = -(-span_rows // 128) * 128
    pieces = 2 if padded % 256 == 0 else 1
    zc = jnp.transpose(transfer_impedance, (0, 2, 1)).reshape(2 * members, outer, span_rows)
    zc = jnp.pad(zc, ((0, 0), (0, 0), (0, padded - span_rows))).reshape(2 * members, outer * padded)

    pad = 128 - lines - convs - ports
    index = jnp.concatenate([line_node, conv_node, port_node, jnp.full((1, pad), -1, jnp.int32)], axis=1)
    ones = jnp.ones((1, 128 - lines - convs), F32)
    coef = jnp.concatenate(
        [
            jnp.concatenate([2.0 * line_admittance, jnp.ones((1, convs), F32), port_admittance, ones[:, :pad]], axis=1),
            jnp.concatenate([jnp.ones((1, lines), F32), conv_rate, ones], axis=1),
            jnp.concatenate([jnp.ones((1, lines), F32), conv_limit, ones], axis=1),
        ],
        axis=0,
    )
    angles = jnp.arange(1, STEPS + 1, dtype=F32) * jnp.float32(2.0 * math.pi / STEPS)
    trig = jnp.stack([jnp.cos(angles), jnp.sin(angles)])
    flops = 2 * STEPS * (nodes + 128) * (2 * nodes + 256) * 256
    waves, hist_end, conv_out, port_voltage, bus_voltage = pl.pallas_call(
        functools.partial(window_kernel, lines, convs, ports),
        out_shape=(
            jax.ShapeDtypeStruct((STEPS, lines, cases), F32),
            jax.ShapeDtypeStruct((nodes, cases), F32),
            jax.ShapeDtypeStruct((2, convs, cases), F32),
            jax.ShapeDtypeStruct((2, ports, cases), F32),
            jax.ShapeDtypeStruct((2, bus_rows, cases), F32),
        ),
        in_specs=[smem()] * 4 + [vmem()] * 12 + [smem(), pl.BlockSpec(memory_space=pl.ANY)],
        out_specs=(vmem(),) * 4 + (pl.BlockSpec(memory_space=pl.ANY),),
        scratch_shapes=[
            pltpu.VMEM((nodes + 128, 2 * nodes + 256), BF16),
            pltpu.VMEM((nodes, 256), BF16),
            pltpu.VMEM((256, 256), BF16),
            pltpu.VMEM((128, nodes), F32),
            pltpu.VMEM((128, 128), F32),
            pltpu.VMEM((2, ports, cases), F32),
            pltpu.VMEM((pieces, areas, 2 * members, padded // pieces), F32),
            pltpu.VMEM((areas, group, 2, ports, cases), F32),
            pltpu.VMEM((2, bus_rows, cases), F32),
            pltpu.VMEM((areas * 2 * members, 2 * cases), F32),
            pltpu.VMEM((areas * 2 * members, 2 * cases), BF16),
            pltpu.VMEM((areas * 2 * members, 2 * cases), BF16),
            pltpu.SemaphoreType.DMA((pieces, outer)),
            pltpu.SemaphoreType.DMA((pieces, areas)),
            pltpu.SemaphoreType.DMA((pieces, outer, inner)),
            pltpu.SemaphoreType.DMA((group,)),
            pltpu.SemaphoreType.DMA((group,)),
            pltpu.SemaphoreType.DMA((areas,)),
            pltpu.SemaphoreType.DMA((areas,)),
            pltpu.SemaphoreType.DMA((pieces,)),
            pltpu.SemaphoreType.DMA((2, SUBS)),
            pltpu.SemaphoreType.DMA((outer, SUBS)),
            pltpu.SemaphoreType.DMA((2, outer, SUBS)),
            pltpu.SemaphoreType.DMA((2, outer, inner, SUBS)),
            pltpu.SemaphoreType.DMA((outer, inner, SUBS)),
            pltpu.SemaphoreType.DMA((2, outer, inner)),
            pltpu.VMEM((group, 2, ports, cases), F32),
            pltpu.VMEM((group, 2, ports, cases), F32),
            pltpu.SemaphoreType.DMA((group,)),
            pltpu.SemaphoreType.DMA((group,)),
        ],
        compiler_params=pltpu.CompilerParams(collective_id=0, has_side_effects=True),
        cost_estimate=pl.CostEstimate(flops=flops, bytes_accessed=8_000_000, transcendentals=0),
        name="window",
    )(
        reach,
        line_delay[0],
        trig,
        conv_count,
        index,
        coef,
        conductance_inverse[0],
        cap_conductance,
        cap_history[0],
        below1,
        below2,
        above1,
        above2,
        conv_state[0],
        conv_reference[0],
        port_voltage_prev[:, 0],
        port_bus.reshape(-1),
        zc,
    )

    return (waves[None], hist_end[None], conv_out[None], bus_voltage, port_voltage[:, None])


def solution(mesh):
    both = ("area", "row")
    placed = (
        P(both, None, None),
        P(both, None, None),
        P(both, None),
        P(both, None, None, None),
        P(both, None),
        P(both, None),
        P(both, None),
        P(both, None),
        P(both, None),
        P(both),
        P(both, None, None, None),
        P(both, None, None, None),
        P(both, None),
        P(both, None),
        P(both, None),
        P(both, None),
        P(None, both, None, None),
        P("area", None),
        P(None, "row", "area"),
    )
    return jax.shard_map(
        per_device,
        mesh=mesh,
        in_specs=placed,
        out_specs=(
            P(both, None, None, None),
            P(both, None, None),
            P(both, None, None, None),
            P(None, "row", None),
            P(None, both, None, None),
        ),
        check_vma=False,
    )
```

```python
import functools
import math

import jax
import jax.numpy as jnp
import numpy as np
from jax import lax
from jax.experimental import pallas as pl
from jax.experimental.pallas import tpu as pltpu
from jax.sharding import PartitionSpec as P

STEPS = 20
SAG_FACTOR = 0.3
F32 = jnp.float32
BF16 = jnp.bfloat16
MESH = pl.DeviceIdType.MESH
SUBS = 10
NEAR = 12


def split(x):
    high = x.astype(BF16)
    return high, (x - high.astype(F32)).astype(BF16)


def mm(a, b):
    return lax.dot_general(a, b, (((1,), (0,)), ((), ())), preferred_element_type=F32)


def columns(row, count):
    return jnp.broadcast_to(row, (128, count)).T


def window_kernel(
    lines,
    convs,
    ports,
    partner_ref,
    delay_ref,
    trig_ref,
    count_ref,
    line_node_ref,
    conv_node_ref,
    port_node_ref,
    line_adm_ref,
    conv_rate_ref,
    conv_limit_ref,
    port_adm_ref,
    ginv_ref,
    gcap_ref,
    hist_ref,
    past_ref,
    state_ref,
    target_ref,
    pvolt_ref,
    port_bus_ref,
    zc_ref,
    waves_ref,
    hist_out_ref,
    state_out_ref,
    port_ref,
    bus_ref,
    big,
    wj,
    wx,
    cap2,
    xs,
    current_ref,
    zin,
    cin,
    vbus,
    flat_ref,
    rh,
    rl,
    zs,
    zr,
    zf,
    rs,
    rr,
    cs,
    cr,
    zlocal,
    os,
    orr,
    fs,
    xf,
    xr,
    olocal,
    picked,
    landed,
    ps,
    pr,
    sorted_out,
    sorted_in,
    base_ref,
    ws,
    wr,
):
    nodes = ginv_ref.shape[0]
    probes = 128
    half = lines // 2
    rows = 256
    areas, group = cin.shape[0], cin.shape[1]
    pieces, depth, width = zin.shape[0], zin.shape[2], zin.shape[3]
    inner = 2 ** ((areas.bit_length() - 1) // 2)
    outer = areas // inner
    span_rows = bus_ref.shape[1] // outer
    chunk = span_rows // inner
    a = lax.axis_index("area")
    r = lax.axis_index("row")
    zi = lax.div(a, inner)
    xi = lax.rem(a, inner)

    def subnet(by):
        to = lax.rem(a * group + r + by + areas * group, areas * group)
        return (lax.div(to, group), lax.rem(to, group))

    barrier = pltpu.get_barrier_semaphore()
    for d in range(1, areas):
        pl.semaphore_signal(barrier, inc=1, device_id=(lax.rem(a + d, areas), r), device_id_type=MESH)
    for d in range(1, group):
        pl.semaphore_signal(barrier, inc=1, device_id=(a, lax.rem(r + d, group)), device_id_type=MESH)
    for by in (1, -1, 2, -2):
        pl.semaphore_signal(barrier, inc=1, device_id=subnet(by), device_id_type=MESH)

    hist_steps = past_ref.shape[0] // lines
    near = []
    place = []
    seen = jnp.int32(0)
    for l in range(half):
        gap = partner_ref[l] - (a * group + r)
        near.append((gap == 1) | (gap == 1 - areas * group))
        place.append(jnp.where(near[l], seen, NEAR + l - seen))
        seen = seen + jnp.where(near[l], 1, 0)
    for l in range(lines):
        start = jnp.clip(hist_steps - delay_ref[l], 0, hist_steps - STEPS)
        base_ref[l] = jnp.clip(place[l % half], 0, half - 1) * hist_steps + start
    for k in range(half):
        line = jnp.int32(0)
        for l in range(half):
            line = line + jnp.where(place[l] == k, l, 0)
        line = jnp.clip(line, 0, half - 1)
        slot = pl.ds(k * hist_steps, hist_steps)
        sorted_out[0, slot, :] = past_ref[pl.ds(line, hist_steps, stride=lines), :]
        sorted_out[1, slot, :] = past_ref[pl.ds(line + half, hist_steps, stride=lines), :]
    pl.semaphore_wait(barrier, areas + group + 2)

    def send(src, dst, ssem, rsem, to):
        return pltpu.make_async_remote_copy(
            src_ref=src, dst_ref=dst, send_sem=ssem, recv_sem=rsem, device_id=to, device_id_type=MESH
        )

    wave_sends = []
    edge = NEAR * hist_steps
    for side, way in enumerate((1, -1)):
        for reach, slots in ((1, pl.ds(0, edge)), (2, pl.ds(edge, half * hist_steps - edge))):
            sem = 2 * side + reach - 1
            copy = send(
                sorted_out.at[side, slots, :], sorted_in.at[side, slots, :], ws.at[sem], wr.at[sem], subnet(way * reach)
            )
            copy.start()
            wave_sends.append(copy)

    def mate(e):
        return zi * inner + lax.rem(xi + e, inner)

    def part_of(plane, p):
        return zc_ref.at[:, pl.ds(pl.multiple_of((plane * pieces + p) * width, 128), width)]

    z_sends = []
    own_z = []
    for p in range(pieces):
        copy = pltpu.make_async_copy(part_of(zi, p), zin.at[p, a], zlocal.at[p])
        copy.start()
        own_z.append(copy)
        for d in range(1, outer):
            plane = lax.rem(zi + d, outer)
            copy = send(part_of(plane, p), zin.at[p, a], zs.at[p, d], zr.at[p, a], (plane * inner + xi, r))
            copy.start()
            z_sends.append(copy)
        for e in range(1, inner):
            copy = send(part_of(zi, p), zin.at[p, a], zf.at[p, 0, e], zr.at[p, a], (mate(e), r))
            copy.start()
            z_sends.append(copy)

    def relay_z(p):
        for d in range(1, outer):
            owner = lax.rem(zi + outer - d, outer) * inner + xi
            block = zin.at[p, owner]
            send(block, block, zs.at[p, d], zr.at[p, owner], (owner, r)).wait_recv()
            for e in range(1, inner):
                copy = send(block, block, zf.at[p, d, e], zr.at[p, owner], (mate(e), r))
                copy.start()
                z_sends.append(copy)

    pad = probes - lines - convs - ports

    def stacked(line, conv, port, rest):
        return jnp.concatenate(
            [columns(line, lines), columns(conv, convs), columns(port, ports), jnp.full((pad, 128), rest, F32)], axis=0
        )

    index = stacked(
        line_node_ref[...].astype(F32), conv_node_ref[...].astype(F32), port_node_ref[...].astype(F32), -1.0
    ).astype(jnp.int32)
    for c in range(nodes // 128):
        lane = lax.broadcasted_iota(jnp.int32, (probes, 128), 1) + 128 * c
        cap2[:, c * 128 : (c + 1) * 128] = jnp.where(index == lane, 1.0, 0.0)
    pick = cap2[...].astype(BF16)
    scatter = cap2[...].T.astype(BF16)
    for b in range(nodes // rows):
        span = pl.ds(b * rows, rows)
        high, low = split(ginv_ref[span, :])
        big[span, 0:nodes] = high
        big[span, nodes : 2 * nodes] = low
    tail = pl.ds(nodes, probes)
    big[tail, :nodes] = mm(pick, big[0:nodes, 0:nodes]).astype(BF16)
    big[tail, nodes : 2 * nodes] = mm(pick, big[0:nodes, nodes : 2 * nodes]).astype(BF16)
    big[:, 2 * nodes : 2 * nodes + 128] = mm(big[:, 0:nodes], scatter).astype(BF16)
    big[:, 2 * nodes + 128 :] = mm(big[:, nodes : 2 * nodes], scatter).astype(BF16)
    gcap = 2.0 * columns(gcap_ref[...], nodes)

    def put_state(value):
        high, low = split(value)
        wj[:, 0:128] = high
        wj[:, 128:256] = low

    hist_out_ref[...] = hist_ref[...]
    put_state(hist_ref[...])
    state_out_ref[...] = state_ref[...]
    current_ref[...] = jnp.zeros_like(current_ref)
    two_adm = 2.0 * columns(line_adm_ref[...], lines)
    rate = columns(conv_rate_ref[...], convs)
    limit = columns(conv_limit_ref[...], convs)
    padm = columns(port_adm_ref[...], ports)
    live = lax.broadcasted_iota(jnp.int32, (convs, 128), 0) < count_ref[0]
    xs[lines + convs + ports :, :] = jnp.zeros((probes - lines - convs - ports, 128), F32)

    def step(t, carry):
        cosine = trig_ref[0, t]
        sine = trig_ref[1, t]
        for l in range(half):
            xs[l : l + 1, :] = sorted_in[1, pl.ds(base_ref[l] + t, 1), :]
            xs[l + half : l + half + 1, :] = sorted_in[0, pl.ds(base_ref[l + half] + t, 1), :]
        inward = xs[0:lines, :]
        axial = state_out_ref[0]
        normal = state_out_ref[1]
        source = padm * (pvolt_ref[0] * cosine - pvolt_ref[1] * sine)
        xs[lines : lines + convs, :] = jnp.where(live, axial * cosine - normal * sine, 0.0)
        xs[lines + convs : lines + convs + ports, :] = source
        high, low = split(xs[...])
        wx[0:128, 0:128] = high
        wx[128:256, 0:128] = high
        wx[0:128, 128:256] = low
        wx[128:256, 128:256] = low

        def apply(start, size):
            span = pl.ds(start, size)
            both = (
                mm(big[span, 0:nodes], wj[...])
                + mm(big[span, nodes : 2 * nodes], wj[...])
                + mm(big[span, 2 * nodes :], wx[...])
            )
            return both[:, 0:128] + both[:, 128:256]

        probe = apply(nodes, probes)
        volts = apply(0, nodes)
        waves_ref[t] = two_adm * probe[0:lines] - inward
        emf = probe[lines : lines + convs]
        flow = source - padm * probe[lines + convs : lines + convs + ports]
        current_ref[0] += flow * cosine
        current_ref[1] -= flow * sine
        new_axial = axial + rate * (target_ref[0] - axial) - SAG_FACTOR * emf * cosine
        new_normal = normal + rate * (target_ref[1] - normal) + SAG_FACTOR * emf * sine
        state_out_ref[0] = jnp.where(live, limit * jnp.tanh(new_axial / limit), axial)
        state_out_ref[1] = jnp.where(live, limit * jnp.tanh(new_normal / limit), normal)
        after = gcap * volts - hist_out_ref[...]
        hist_out_ref[...] = after
        put_state(after)
        return carry

    for copy in wave_sends:
        copy.wait()

    stops = [STEPS * 9 // 10 - (pieces - 1 - p) * STEPS * 2 // 5 for p in range(pieces)]
    at = 0
    for p, stop in enumerate(stops):
        lax.fori_loop(at, stop, step, 0)
        relay_z(p)
        at = stop
    lax.fori_loop(at, STEPS, step, 0)
    cin[a, r] = current_ref[...] * (2.0 / STEPS)

    copies = []
    for d in range(1, group):
        block = cin.at[a, r]
        copy = send(block, block, rs.at[d], rr.at[d], (a, lax.rem(r + d, group)))
        copy.start()
        copies.append(copy)
    for copy in copies:
        copy.wait()
    copies = []
    for d in range(1, areas):
        block = cin.at[a]
        copy = send(block, block, cs.at[d], cr.at[d], (lax.rem(a + d, areas), r))
        copy.start()
        copies.append(copy)
    for copy in copies:
        copy.wait()
    members = group * ports
    for i in range(areas):
        for j in range(group):
            re, im = cin[i, j, 0], cin[i, j, 1]
            top = i * depth + j * ports
            flat_ref[top : top + ports, 0:128] = re
            flat_ref[top : top + ports, 128:256] = im
            flat_ref[top + members : top + members + ports, 0:128] = -im
            flat_ref[top + members : top + members + ports, 128:256] = re
    high, low = split(flat_ref[...])
    rh[...] = high
    rl[...] = low

    for p in range(pieces):
        own_z[p].wait()
    for copy in z_sends:
        copy.wait_send()
    for p in range(pieces):
        for e in range(1, inner):
            for q in range(outer):
                owner = q * inner + lax.rem(xi + e, inner)
                block = zin.at[p, owner]
                send(block, block, zf.at[p, 0, e], zr.at[p, owner], (owner, r)).wait_recv()

    def product(p):
        high, low = split(zin[p].reshape(areas * depth, width).T)
        total = mm(high, rh[...]) + mm(low, rh[...]) + mm(high, rl[...])
        keep = min(width, span_rows)
        rows = pl.ds(pl.multiple_of(zi * span_rows + p * width, 8), keep)
        vbus[0, rows, :] = total[:keep, 0:128]
        vbus[1, rows, :] = total[:keep, 128:256]

    cuts = SUBS
    sub = chunk // cuts

    def region(plane, x, k):
        top = pl.multiple_of(plane * span_rows + x * chunk + k * sub, 8)
        return vbus.at[:, pl.ds(top, sub), :]

    def emit(plane, x, count, sem):
        rows = pl.ds(pl.multiple_of(plane * span_rows + x * chunk, 8), count)
        return pltpu.make_async_copy(vbus.at[:, rows, :], bus_ref.at[:, rows, :], sem)

    def plane_at(plane):
        return (plane * inner + xi, r)

    can_up = zi + 1 < outer
    can_down = zi >= 1

    def launch(k):
        up = send(region(zi, xi, k), region(zi, xi, k), os.at[0, k], orr.at[zi, k], plane_at(zi + 1))
        down = send(region(zi, xi, k), region(zi, xi, k), os.at[1, k], orr.at[zi, k], plane_at(zi - 1))
        return up, down

    if pieces == inner:
        product(xi)
    else:
        for p in range(pieces):
            product(p)
    for k in range(cuts):
        up, down = launch(k)
        pl.when(can_up)(up.start)
        pl.when(can_down)(down.start)
    if pieces == inner:
        for i in range(1, pieces):
            product(lax.rem(xi + i, inner))
    local = emit(zi, 0, span_rows, olocal.at[0, 0, 0])
    local.start()

    def hops(d):
        return ((zi - d, zi - d >= 0, zi + 1, can_up), (zi + d, zi + d < outer, zi - 1, can_down))

    def relay(plane, k, d, side, ahead):
        block = region(plane, xi, k)
        onward = send(block, block, fs.at[side, d, k], orr.at[plane, k], plane_at(ahead))
        across = [
            send(block, block, xf.at[side, d, e, k], xr.at[plane, xi, k], (mate(e), r)) for e in range(1, inner)
        ]
        return onward, across

    for d in range(1, outer):
        for k in range(cuts):
            for side, (plane, have, ahead, go) in enumerate(hops(d)):

                @pl.when(have)
                def _(plane=plane, k=k, d=d, side=side, ahead=ahead, go=go):
                    onward, across = relay(plane, k, d, side, ahead)
                    onward.wait_recv()
                    pl.when(go)(onward.start)
                    for copy in across:
                        copy.start()

    for d in range(1, outer):
        for side, (plane, have, ahead, go) in enumerate(hops(d)):

            @pl.when(have)
            def _(plane=plane, d=d, side=side):
                emit(plane, xi, chunk, olocal.at[side, d, 0]).start()
                for e in range(1, inner):
                    x = lax.rem(xi + e, inner)
                    for k in range(cuts):
                        block = region(plane, x, k)
                        send(block, block, xf.at[side, d, e, k], xr.at[plane, x, k], (mate(e), r)).wait_recv()
                    emit(plane, x, chunk, olocal.at[side, d, e]).start()

    members = port_bus_ref.shape[0] // group
    for j in range(group):
        for p in range(members):
            place = port_bus_ref[j * members + p] - r * bus_ref.shape[1]
            inside = (place >= 0) & (place < bus_ref.shape[1])
            place = jnp.clip(place, 0, bus_ref.shape[1] - 1)
            for part in range(2):
                value = vbus[part, pl.ds(place, 1), :]
                picked[j, part, p : p + 1, :] = jnp.where(inside, value, 0.0)

    def hand(d):
        to = lax.rem(r + d, group)
        return send(picked.at[to], landed.at[r], ps.at[d], pr.at[d], (a, to))

    for d in range(1, group):
        hand(d).start()
    for d in range(1, outer):
        for side, (plane, have, ahead, go) in enumerate(hops(d)):

            @pl.when(have)
            def _(plane=plane, d=d, side=side, ahead=ahead, go=go):
                for k in range(cuts):
                    onward, across = relay(plane, k, d, side, ahead)
                    pl.when(go)(onward.wait_send)
                    for copy in across:
                        copy.wait_send()
                for e in range(inner):
                    emit(plane, lax.rem(xi + e, inner), chunk, olocal.at[side, d, e]).wait()

    for k in range(cuts):
        up, down = launch(k)
        pl.when(can_up)(up.wait_send)
        pl.when(can_down)(down.wait_send)
    for d in range(1, group):
        hand(d).wait()
    value = picked[r]
    for d in range(1, group):
        value = value + landed[lax.rem(r + d, group)]
    port_ref[...] = value
    local.wait()


def vmem():
    return pl.BlockSpec(memory_space=pltpu.VMEM)


def smem():
    return pl.BlockSpec(memory_space=pltpu.SMEM)


def per_device(
    conductance_inverse,
    cap_history,
    cap_conductance,
    wave_history,
    line_partner,
    line_node,
    line_delay,
    line_admittance,
    conv_node,
    conv_count,
    conv_state,
    conv_reference,
    conv_rate,
    conv_limit,
    port_node,
    port_admittance,
    port_voltage_prev,
    port_bus,
    transfer_impedance,
):
    steps_kept, lines, cases = wave_history.shape[1:]
    nodes = conductance_inverse.shape[1]
    convs = conv_node.shape[1]
    ports = port_node.shape[1]
    areas = lax.axis_size("area")
    group = lax.axis_size("row")
    bus_rows = transfer_impedance.shape[1]
    members = transfer_impedance.shape[2]
    inner = 2 ** ((areas.bit_length() - 1) // 2)
    outer = areas // inner
    span_rows = bus_rows // outer
    padded = -(-span_rows // 128) * 128
    pieces = 2 if padded % 256 == 0 else 1
    zc = jnp.transpose(transfer_impedance, (0, 2, 1)).reshape(2 * members, outer, span_rows)
    zc = jnp.pad(zc, ((0, 0), (0, 0), (0, padded - span_rows))).reshape(2 * members, outer * padded)

    angles = np.arange(1, STEPS + 1, dtype=np.float32) * np.float32(2.0 * math.pi / STEPS)
    trig = jnp.asarray(np.stack([np.cos(angles), np.sin(angles)]).astype(np.float32))
    flops = 2 * STEPS * (nodes + 128) * (2 * nodes + 256) * 256
    waves, hist_end, conv_out, port_voltage, bus_voltage = pl.pallas_call(
        functools.partial(window_kernel, lines, convs, ports),
        out_shape=(
            jax.ShapeDtypeStruct((STEPS, lines, cases), F32),
            jax.ShapeDtypeStruct((nodes, cases), F32),
            jax.ShapeDtypeStruct((2, convs, cases), F32),
            jax.ShapeDtypeStruct((2, ports, cases), F32),
            jax.ShapeDtypeStruct((2, bus_rows, cases), F32),
        ),
        in_specs=[smem()] * 4 + [vmem()] * 14 + [smem(), pl.BlockSpec(memory_space=pl.ANY)],
        out_specs=(vmem(),) * 4 + (pl.BlockSpec(memory_space=pl.ANY),),
        scratch_shapes=[
            pltpu.VMEM((nodes + 128, 2 * nodes + 256), BF16),
            pltpu.VMEM((nodes, 256), BF16),
            pltpu.VMEM((256, 256), BF16),
            pltpu.VMEM((128, nodes), F32),
            pltpu.VMEM((128, 128), F32),
            pltpu.VMEM((2, ports, cases), F32),
            pltpu.VMEM((pieces, areas, 2 * members, padded // pieces), F32),
            pltpu.VMEM((areas, group, 2, ports, cases), F32),
            pltpu.VMEM((2, bus_rows, cases), F32),
            pltpu.VMEM((areas * 2 * members, 2 * cases), F32),
            pltpu.VMEM((areas * 2 * members, 2 * cases), BF16),
            pltpu.VMEM((areas * 2 * members, 2 * cases), BF16),
            pltpu.SemaphoreType.DMA((pieces, outer)),
            pltpu.SemaphoreType.DMA((pieces, areas)),
            pltpu.SemaphoreType.DMA((pieces, outer, inner)),
            pltpu.SemaphoreType.DMA((group,)),
            pltpu.SemaphoreType.DMA((group,)),
            pltpu.SemaphoreType.DMA((areas,)),
            pltpu.SemaphoreType.DMA((areas,)),
            pltpu.SemaphoreType.DMA((pieces,)),
            pltpu.SemaphoreType.DMA((2, SUBS)),
            pltpu.SemaphoreType.DMA((outer, SUBS)),
            pltpu.SemaphoreType.DMA((2, outer, SUBS)),
            pltpu.SemaphoreType.DMA((2, outer, inner, SUBS)),
            pltpu.SemaphoreType.DMA((outer, inner, SUBS)),
            pltpu.SemaphoreType.DMA((2, outer, inner)),
            pltpu.VMEM((group, 2, ports, cases), F32),
            pltpu.VMEM((group, 2, ports, cases), F32),
            pltpu.SemaphoreType.DMA((group,)),
            pltpu.SemaphoreType.DMA((group,)),
            pltpu.VMEM((2, lines // 2 * steps_kept, cases), F32),
            pltpu.VMEM((2, lines // 2 * steps_kept, cases), F32),
            pltpu.SMEM((lines,), jnp.int32),
            pltpu.SemaphoreType.DMA((4,)),
            pltpu.SemaphoreType.DMA((4,)),
        ],
        compiler_params=pltpu.CompilerParams(collective_id=0, has_side_effects=True),
        cost_estimate=pl.CostEstimate(flops=flops, bytes_accessed=8_000_000, transcendentals=0),
        name="window",
    )(
        line_partner[0],
        line_delay[0],
        trig,
        conv_count,
        line_node,
        conv_node,
        port_node,
        line_admittance,
        conv_rate,
        conv_limit,
        port_admittance,
        conductance_inverse[0],
        cap_conductance,
        cap_history[0],
        wave_history.reshape(steps_kept * lines, cases),
        conv_state[0],
        conv_reference[0],
        port_voltage_prev[:, 0],
        port_bus.reshape(-1),
        zc,
    )

    return (waves[None], hist_end[None], conv_out[None], bus_voltage, port_voltage[:, None])


def solution(mesh):
    both = ("area", "row")
    placed = (
        P(both, None, None),
        P(both, None, None),
        P(both, None),
        P(both, None, None, None),
        P(both, None),
        P(both, None),
        P(both, None),
        P(both, None),
        P(both, None),
        P(both),
        P(both, None, None, None),
        P(both, None, None, None),
        P(both, None),
        P(both, None),
        P(both, None),
        P(both, None),
        P(None, both, None, None),
        P("area", None),
        P(None, "row", "area"),
    )
    return jax.shard_map(
        per_device,
        mesh=mesh,
        in_specs=placed,
        out_specs=(
            P(both, None, None, None),
            P(both, None, None),
            P(both, None, None, None),
            P(None, "row", None),
            P(None, both, None, None),
        ),
        check_vma=False,
    )
```

```python
import functools
import math

import jax
import jax.numpy as jnp
import numpy as np
from jax import lax
from jax.experimental import pallas as pl
from jax.experimental.pallas import tpu as pltpu
from jax.sharding import PartitionSpec as P

STEPS = 20
SAG_FACTOR = 0.3
F32 = jnp.float32
BF16 = jnp.bfloat16
MESH = pl.DeviceIdType.MESH
SUBS = 10
NEAR = 12
EARLY = 24


def split(x):
    high = x.astype(BF16)
    return high, (x - high.astype(F32)).astype(BF16)


def mm(a, b):
    return lax.dot_general(a, b, (((1,), (0,)), ((), ())), preferred_element_type=F32)


def columns(row, count):
    return jnp.broadcast_to(row, (128, count)).T


def window_kernel(
    lines,
    convs,
    ports,
    partner_ref,
    delay_ref,
    trig_ref,
    count_ref,
    line_node_ref,
    conv_node_ref,
    port_node_ref,
    line_adm_ref,
    conv_rate_ref,
    conv_limit_ref,
    port_adm_ref,
    ginv_ref,
    gcap_ref,
    hist_ref,
    past_ref,
    state_ref,
    target_ref,
    pvolt_ref,
    port_bus_ref,
    zc_ref,
    waves_ref,
    hist_out_ref,
    state_out_ref,
    port_ref,
    bus_ref,
    big,
    wj,
    wx,
    cap2,
    xs,
    current_ref,
    zin,
    cin,
    vbus,
    flat_ref,
    rh,
    rl,
    zs,
    zr,
    zf,
    rs,
    rr,
    cs,
    cr,
    zlocal,
    os,
    orr,
    fs,
    xf,
    xr,
    olocal,
    picked,
    landed,
    ps,
    pr,
    out_early,
    out_late,
    in_early,
    in_late,
    base_ref,
    ws,
    wr,
):
    nodes = ginv_ref.shape[0]
    probes = 128
    half = lines // 2
    rows = 256
    areas, group = cin.shape[0], cin.shape[1]
    pieces, depth, width = zin.shape[0], zin.shape[2], zin.shape[3]
    inner = 2 ** ((areas.bit_length() - 1) // 2)
    outer = areas // inner
    span_rows = bus_ref.shape[1] // outer
    chunk = span_rows // inner
    a = lax.axis_index("area")
    r = lax.axis_index("row")
    zi = lax.div(a, inner)
    xi = lax.rem(a, inner)

    def subnet(by):
        to = lax.rem(a * group + r + by + areas * group, areas * group)
        return (lax.div(to, group), lax.rem(to, group))

    barrier = pltpu.get_barrier_semaphore()
    for d in range(1, areas):
        pl.semaphore_signal(barrier, inc=1, device_id=(lax.rem(a + d, areas), r), device_id_type=MESH)
    for d in range(1, group):
        pl.semaphore_signal(barrier, inc=1, device_id=(a, lax.rem(r + d, group)), device_id_type=MESH)
    for by in (1, -1, 2, -2):
        pl.semaphore_signal(barrier, inc=1, device_id=subnet(by), device_id_type=MESH)

    hist_steps = past_ref.shape[0] // lines
    late = hist_steps - EARLY
    pieces_of = (((out_early, in_early), 0, EARLY), ((out_late, in_late), EARLY, late))
    near = []
    place = []
    seen = jnp.int32(0)
    for l in range(half):
        gap = partner_ref[l] - (a * group + r)
        near.append((gap == 1) | (gap == 1 - areas * group))
        place.append(jnp.where(near[l], seen, NEAR + l - seen))
        seen = seen + jnp.where(near[l], 1, 0)
    for l in range(lines):
        start = jnp.clip(hist_steps - delay_ref[l], 0, hist_steps - STEPS)
        base_ref[0, l] = jnp.clip(place[l % half], 0, half - 1)
        base_ref[1, l] = start
    for k in range(half):
        line = jnp.int32(0)
        for l in range(half):
            line = line + jnp.where(place[l] == k, l, 0)
        line = jnp.clip(line, 0, half - 1)
        for side in range(2):
            for piece, (kept, first, count) in enumerate(pieces_of):
                source = pl.ds(first * lines + side * half + line, count, stride=lines)
                kept[0][side, k * count : (k + 1) * count, :] = past_ref[source, :]
    pl.semaphore_wait(barrier, areas + group + 2)

    def send(src, dst, ssem, rsem, to):
        return pltpu.make_async_remote_copy(
            src_ref=src, dst_ref=dst, send_sem=ssem, recv_sem=rsem, device_id=to, device_id_type=MESH
        )

    def wave_send(piece):
        (out, into), _, count = pieces_of[piece]
        copies = []
        for side, way in enumerate((1, -1)):
            for reach, slots in ((1, pl.ds(0, NEAR * count)), (2, pl.ds(NEAR * count, (half - NEAR) * count))):
                sem = (piece, 2 * side + reach - 1)
                copy = send(
                    out.at[side, slots, :], into.at[side, slots, :], ws.at[sem], wr.at[sem], subnet(way * reach)
                )
                copy.start()
                copies.append(copy)
        return copies

    early_sends = wave_send(0)
    late_sends = wave_send(1)

    def mate(e):
        return zi * inner + lax.rem(xi + e, inner)

    def part_of(plane, p):
        return zc_ref.at[:, pl.ds(pl.multiple_of((plane * pieces + p) * width, 128), width)]

    z_sends = []
    own_z = []
    for p in range(pieces):
        copy = pltpu.make_async_copy(part_of(zi, p), zin.at[p, a], zlocal.at[p])
        copy.start()
        own_z.append(copy)
        for d in range(1, outer):
            plane = lax.rem(zi + d, outer)
            copy = send(part_of(plane, p), zin.at[p, a], zs.at[p, d], zr.at[p, a], (plane * inner + xi, r))
            copy.start()
            z_sends.append(copy)
        for e in range(1, inner):
            copy = send(part_of(zi, p), zin.at[p, a], zf.at[p, 0, e], zr.at[p, a], (mate(e), r))
            copy.start()
            z_sends.append(copy)

    def relay_z(p):
        for d in range(1, outer):
            owner = lax.rem(zi + outer - d, outer) * inner + xi
            block = zin.at[p, owner]
            send(block, block, zs.at[p, d], zr.at[p, owner], (owner, r)).wait_recv()
            for e in range(1, inner):
                copy = send(block, block, zf.at[p, d, e], zr.at[p, owner], (mate(e), r))
                copy.start()
                z_sends.append(copy)

    pad = probes - lines - convs - ports

    def stacked(line, conv, port, rest):
        return jnp.concatenate(
            [columns(line, lines), columns(conv, convs), columns(port, ports), jnp.full((pad, 128), rest, F32)], axis=0
        )

    index = stacked(
        line_node_ref[...].astype(F32), conv_node_ref[...].astype(F32), port_node_ref[...].astype(F32), -1.0
    ).astype(jnp.int32)
    for c in range(nodes // 128):
        lane = lax.broadcasted_iota(jnp.int32, (probes, 128), 1) + 128 * c
        cap2[:, c * 128 : (c + 1) * 128] = jnp.where(index == lane, 1.0, 0.0)
    pick = cap2[...].astype(BF16)
    scatter = cap2[...].T.astype(BF16)
    for b in range(nodes // rows):
        span = pl.ds(b * rows, rows)
        high, low = split(ginv_ref[span, :])
        big[span, 0:nodes] = high
        big[span, nodes : 2 * nodes] = low
    tail = pl.ds(nodes, probes)
    big[tail, :nodes] = mm(pick, big[0:nodes, 0:nodes]).astype(BF16)
    big[tail, nodes : 2 * nodes] = mm(pick, big[0:nodes, nodes : 2 * nodes]).astype(BF16)
    big[:, 2 * nodes : 2 * nodes + 128] = mm(big[:, 0:nodes], scatter).astype(BF16)
    big[:, 2 * nodes + 128 :] = mm(big[:, nodes : 2 * nodes], scatter).astype(BF16)
    gcap = 2.0 * columns(gcap_ref[...], nodes)

    def put_state(value):
        high, low = split(value)
        wj[:, 0:128] = high
        wj[:, 128:256] = low

    hist_out_ref[...] = hist_ref[...]
    put_state(hist_ref[...])
    state_out_ref[...] = state_ref[...]
    current_ref[...] = jnp.zeros_like(current_ref)
    two_adm = 2.0 * columns(line_adm_ref[...], lines)
    rate = columns(conv_rate_ref[...], convs)
    limit = columns(conv_limit_ref[...], convs)
    padm = columns(port_adm_ref[...], ports)
    live = lax.broadcasted_iota(jnp.int32, (convs, 128), 0) < count_ref[0]
    xs[lines + convs + ports :, :] = jnp.zeros((probes - lines - convs - ports, 128), F32)

    def advance(both, t, carry):
        cosine = trig_ref[0, t]
        sine = trig_ref[1, t]
        for l in range(lines):
            side = 1 if l < half else 0
            slot = base_ref[0, l]
            when = base_ref[1, l] + t
            row = in_early[side, pl.ds(slot * EARLY + jnp.minimum(when, EARLY - 1), 1), :]
            if both:
                other = in_late[side, pl.ds(slot * late + jnp.maximum(when - EARLY, 0), 1), :]
                row = jnp.where(when < EARLY, row, other)
            xs[l : l + 1, :] = row
        inward = xs[0:lines, :]
        axial = state_out_ref[0]
        normal = state_out_ref[1]
        source = padm * (pvolt_ref[0] * cosine - pvolt_ref[1] * sine)
        xs[lines : lines + convs, :] = jnp.where(live, axial * cosine - normal * sine, 0.0)
        xs[lines + convs : lines + convs + ports, :] = source
        high, low = split(xs[...])
        wx[0:128, 0:128] = high
        wx[128:256, 0:128] = high
        wx[0:128, 128:256] = low
        wx[128:256, 128:256] = low

        def apply(start, size):
            span = pl.ds(start, size)
            both = (
                mm(big[span, 0:nodes], wj[...])
                + mm(big[span, nodes : 2 * nodes], wj[...])
                + mm(big[span, 2 * nodes :], wx[...])
            )
            return both[:, 0:128] + both[:, 128:256]

        probe = apply(nodes, probes)
        volts = apply(0, nodes)
        waves_ref[t] = two_adm * probe[0:lines] - inward
        emf = probe[lines : lines + convs]
        flow = source - padm * probe[lines + convs : lines + convs + ports]
        current_ref[0] += flow * cosine
        current_ref[1] -= flow * sine
        new_axial = axial + rate * (target_ref[0] - axial) - SAG_FACTOR * emf * cosine
        new_normal = normal + rate * (target_ref[1] - normal) + SAG_FACTOR * emf * sine
        state_out_ref[0] = jnp.where(live, limit * jnp.tanh(new_axial / limit), axial)
        state_out_ref[1] = jnp.where(live, limit * jnp.tanh(new_normal / limit), normal)
        after = gcap * volts - hist_out_ref[...]
        hist_out_ref[...] = after
        put_state(after)
        return carry

    for copy in early_sends:
        copy.wait()
    at = EARLY - hist_steps + STEPS
    lax.fori_loop(0, at, functools.partial(advance, False), 0)
    for copy in late_sends:
        copy.wait()
    step = functools.partial(advance, True)
    stops = [STEPS * 9 // 10 - (pieces - 1 - p) * STEPS * 2 // 5 for p in range(pieces)]
    for p, stop in enumerate(stops):
        lax.fori_loop(at, stop, step, 0)
        relay_z(p)
        at = stop
    lax.fori_loop(at, STEPS, step, 0)
    cin[a, r] = current_ref[...] * (2.0 / STEPS)

    copies = []
    for d in range(1, group):
        block = cin.at[a, r]
        copy = send(block, block, rs.at[d], rr.at[d], (a, lax.rem(r + d, group)))
        copy.start()
        copies.append(copy)
    for copy in copies:
        copy.wait()
    copies = []
    for d in range(1, areas):
        block = cin.at[a]
        copy = send(block, block, cs.at[d], cr.at[d], (lax.rem(a + d, areas), r))
        copy.start()
        copies.append(copy)
    for copy in copies:
        copy.wait()
    members = group * ports
    for i in range(areas):
        for j in range(group):
            re, im = cin[i, j, 0], cin[i, j, 1]
            top = i * depth + j * ports
            flat_ref[top : top + ports, 0:128] = re
            flat_ref[top : top + ports, 128:256] = im
            flat_ref[top + members : top + members + ports, 0:128] = -im
            flat_ref[top + members : top + members + ports, 128:256] = re
    high, low = split(flat_ref[...])
    rh[...] = high
    rl[...] = low

    for p in range(pieces):
        own_z[p].wait()
    for copy in z_sends:
        copy.wait_send()
    for p in range(pieces):
        for e in range(1, inner):
            for q in range(outer):
                owner = q * inner + lax.rem(xi + e, inner)
                block = zin.at[p, owner]
                send(block, block, zf.at[p, 0, e], zr.at[p, owner], (owner, r)).wait_recv()

    def product(p):
        high, low = split(zin[p].reshape(areas * depth, width).T)
        total = mm(high, rh[...]) + mm(low, rh[...]) + mm(high, rl[...])
        keep = min(width, span_rows)
        rows = pl.ds(pl.multiple_of(zi * span_rows + p * width, 8), keep)
        vbus[0, rows, :] = total[:keep, 0:128]
        vbus[1, rows, :] = total[:keep, 128:256]

    cuts = SUBS
    sub = chunk // cuts

    def region(plane, x, k):
        top = pl.multiple_of(plane * span_rows + x * chunk + k * sub, 8)
        return vbus.at[:, pl.ds(top, sub), :]

    def emit(plane, x, count, sem):
        rows = pl.ds(pl.multiple_of(plane * span_rows + x * chunk, 8), count)
        return pltpu.make_async_copy(vbus.at[:, rows, :], bus_ref.at[:, rows, :], sem)

    def plane_at(plane):
        return (plane * inner + xi, r)

    can_up = zi + 1 < outer
    can_down = zi >= 1

    def launch(k):
        up = send(region(zi, xi, k), region(zi, xi, k), os.at[0, k], orr.at[zi, k], plane_at(zi + 1))
        down = send(region(zi, xi, k), region(zi, xi, k), os.at[1, k], orr.at[zi, k], plane_at(zi - 1))
        return up, down

    if pieces == inner:
        product(xi)
    else:
        for p in range(pieces):
            product(p)
    for k in range(cuts):
        up, down = launch(k)
        pl.when(can_up)(up.start)
        pl.when(can_down)(down.start)
    if pieces == inner:
        for i in range(1, pieces):
            product(lax.rem(xi + i, inner))
    local = emit(zi, 0, span_rows, olocal.at[0, 0, 0])
    local.start()

    def hops(d):
        return ((zi - d, zi - d >= 0, zi + 1, can_up), (zi + d, zi + d < outer, zi - 1, can_down))

    def relay(plane, k, d, side, ahead):
        block = region(plane, xi, k)
        onward = send(block, block, fs.at[side, d, k], orr.at[plane, k], plane_at(ahead))
        across = [
            send(block, block, xf.at[side, d, e, k], xr.at[plane, xi, k], (mate(e), r)) for e in range(1, inner)
        ]
        return onward, across

    for d in range(1, outer):
        for k in range(cuts):
            for side, (plane, have, ahead, go) in enumerate(hops(d)):

                @pl.when(have)
                def _(plane=plane, k=k, d=d, side=side, ahead=ahead, go=go):
                    onward, across = relay(plane, k, d, side, ahead)
                    onward.wait_recv()
                    pl.when(go)(onward.start)
                    for copy in across:
                        copy.start()

    for d in range(1, outer):
        for side, (plane, have, ahead, go) in enumerate(hops(d)):

            @pl.when(have)
            def _(plane=plane, d=d, side=side):
                emit(plane, xi, chunk, olocal.at[side, d, 0]).start()
                for e in range(1, inner):
                    x = lax.rem(xi + e, inner)
                    for k in range(cuts):
                        block = region(plane, x, k)
                        send(block, block, xf.at[side, d, e, k], xr.at[plane, x, k], (mate(e), r)).wait_recv()
                    emit(plane, x, chunk, olocal.at[side, d, e]).start()

    members = port_bus_ref.shape[1]
    for j in range(group):
        for p in range(members):
            place = port_bus_ref[j, p] - r * bus_ref.shape[1]
            inside = (place >= 0) & (place < bus_ref.shape[1])
            place = jnp.clip(place, 0, bus_ref.shape[1] - 1)
            for part in range(2):
                value = vbus[part, pl.ds(place, 1), :]
                picked[j, part, p : p + 1, :] = jnp.where(inside, value, 0.0)

    def hand(d):
        to = lax.rem(r + d, group)
        return send(picked.at[to], landed.at[r], ps.at[d], pr.at[d], (a, to))

    for d in range(1, group):
        hand(d).start()
    for d in range(1, outer):
        for side, (plane, have, ahead, go) in enumerate(hops(d)):

            @pl.when(have)
            def _(plane=plane, d=d, side=side, ahead=ahead, go=go):
                for k in range(cuts):
                    onward, across = relay(plane, k, d, side, ahead)
                    pl.when(go)(onward.wait_send)
                    for copy in across:
                        copy.wait_send()
                for e in range(inner):
                    emit(plane, lax.rem(xi + e, inner), chunk, olocal.at[side, d, e]).wait()

    for k in range(cuts):
        up, down = launch(k)
        pl.when(can_up)(up.wait_send)
        pl.when(can_down)(down.wait_send)
    for d in range(1, group):
        hand(d).wait()
    value = picked[r]
    for d in range(1, group):
        value = value + landed[lax.rem(r + d, group)]
    port_ref[...] = value
    local.wait()


def vmem():
    return pl.BlockSpec(memory_space=pltpu.VMEM)


def smem():
    return pl.BlockSpec(memory_space=pltpu.SMEM)


def per_device(
    conductance_inverse,
    cap_history,
    cap_conductance,
    wave_history,
    line_partner,
    line_node,
    line_delay,
    line_admittance,
    conv_node,
    conv_count,
    conv_state,
    conv_reference,
    conv_rate,
    conv_limit,
    port_node,
    port_admittance,
    port_voltage_prev,
    port_bus,
    transfer_impedance,
):
    steps_kept, lines, cases = wave_history.shape[1:]
    nodes = conductance_inverse.shape[1]
    convs = conv_node.shape[1]
    ports = port_node.shape[1]
    areas = lax.axis_size("area")
    group = lax.axis_size("row")
    bus_rows = transfer_impedance.shape[1]
    members = transfer_impedance.shape[2]
    inner = 2 ** ((areas.bit_length() - 1) // 2)
    outer = areas // inner
    span_rows = bus_rows // outer
    padded = -(-span_rows // 128) * 128
    pieces = 2 if padded % 256 == 0 else 1
    zc = jnp.transpose(transfer_impedance, (0, 2, 1)).reshape(2 * members, outer, span_rows)
    zc = jnp.pad(zc, ((0, 0), (0, 0), (0, padded - span_rows))).reshape(2 * members, outer * padded)

    angles = np.arange(1, STEPS + 1, dtype=np.float32) * np.float32(2.0 * math.pi / STEPS)
    trig = jnp.asarray(np.stack([np.cos(angles), np.sin(angles)]).astype(np.float32))
    flops = 2 * STEPS * (nodes + 128) * (2 * nodes + 256) * 256
    waves, hist_end, conv_out, port_voltage, bus_voltage = pl.pallas_call(
        functools.partial(window_kernel, lines, convs, ports),
        out_shape=(
            jax.ShapeDtypeStruct((STEPS, lines, cases), F32),
            jax.ShapeDtypeStruct((nodes, cases), F32),
            jax.ShapeDtypeStruct((2, convs, cases), F32),
            jax.ShapeDtypeStruct((2, ports, cases), F32),
            jax.ShapeDtypeStruct((2, bus_rows, cases), F32),
        ),
        in_specs=[smem()] * 4 + [vmem()] * 14 + [smem(), pl.BlockSpec(memory_space=pl.ANY)],
        out_specs=(vmem(),) * 4 + (pl.BlockSpec(memory_space=pl.ANY),),
        scratch_shapes=[
            pltpu.VMEM((nodes + 128, 2 * nodes + 256), BF16),
            pltpu.VMEM((nodes, 256), BF16),
            pltpu.VMEM((256, 256), BF16),
            pltpu.VMEM((128, nodes), F32),
            pltpu.VMEM((128, 128), F32),
            pltpu.VMEM((2, ports, cases), F32),
            pltpu.VMEM((pieces, areas, 2 * members, padded // pieces), F32),
            pltpu.VMEM((areas, group, 2, ports, cases), F32),
            pltpu.VMEM((2, bus_rows, cases), F32),
            pltpu.VMEM((areas * 2 * members, 2 * cases), F32),
            pltpu.VMEM((areas * 2 * members, 2 * cases), BF16),
            pltpu.VMEM((areas * 2 * members, 2 * cases), BF16),
            pltpu.SemaphoreType.DMA((pieces, outer)),
            pltpu.SemaphoreType.DMA((pieces, areas)),
            pltpu.SemaphoreType.DMA((pieces, outer, inner)),
            pltpu.SemaphoreType.DMA((group,)),
            pltpu.SemaphoreType.DMA((group,)),
            pltpu.SemaphoreType.DMA((areas,)),
            pltpu.SemaphoreType.DMA((areas,)),
            pltpu.SemaphoreType.DMA((pieces,)),
            pltpu.SemaphoreType.DMA((2, SUBS)),
            pltpu.SemaphoreType.DMA((outer, SUBS)),
            pltpu.SemaphoreType.DMA((2, outer, SUBS)),
            pltpu.SemaphoreType.DMA((2, outer, inner, SUBS)),
            pltpu.SemaphoreType.DMA((outer, inner, SUBS)),
            pltpu.SemaphoreType.DMA((2, outer, inner)),
            pltpu.VMEM((group, 2, ports, cases), F32),
            pltpu.VMEM((group, 2, ports, cases), F32),
            pltpu.SemaphoreType.DMA((group,)),
            pltpu.SemaphoreType.DMA((group,)),
            pltpu.VMEM((2, lines // 2 * EARLY, cases), F32),
            pltpu.VMEM((2, lines // 2 * (steps_kept - EARLY), cases), F32),
            pltpu.VMEM((2, lines // 2 * EARLY, cases), F32),
            pltpu.VMEM((2, lines // 2 * (steps_kept - EARLY), cases), F32),
            pltpu.SMEM((2, lines), jnp.int32),
            pltpu.SemaphoreType.DMA((2, 4)),
            pltpu.SemaphoreType.DMA((2, 4)),
        ],
        compiler_params=pltpu.CompilerParams(collective_id=0, has_side_effects=True),
        cost_estimate=pl.CostEstimate(flops=flops, bytes_accessed=8_000_000, transcendentals=0),
        name="window",
    )(
        line_partner[0],
        line_delay[0],
        trig,
        conv_count,
        line_node,
        conv_node,
        port_node,
        line_admittance,
        conv_rate,
        conv_limit,
        port_admittance,
        conductance_inverse[0],
        cap_conductance,
        cap_history[0],
        wave_history.reshape(steps_kept * lines, cases),
        conv_state[0],
        conv_reference[0],
        port_voltage_prev[:, 0],
        port_bus,
        zc,
    )

    return (waves[None], hist_end[None], conv_out[None], bus_voltage, port_voltage[:, None])


def solution(mesh):
    both = ("area", "row")
    placed = (
        P(both, None, None),
        P(both, None, None),
        P(both, None),
        P(both, None, None, None),
        P(both, None),
        P(both, None),
        P(both, None),
        P(both, None),
        P(both, None),
        P(both),
        P(both, None, None, None),
        P(both, None, None, None),
        P(both, None),
        P(both, None),
        P(both, None),
        P(both, None),
        P(None, both, None, None),
        P("area", None),
        P(None, "row", "area"),
    )
    return jax.shard_map(
        per_device,
        mesh=mesh,
        in_specs=placed,
        out_specs=(
            P(both, None, None, None),
            P(both, None, None),
            P(both, None, None, None),
            P(None, "row", None),
            P(None, both, None, None),
        ),
        check_vma=False,
    )
```

```python
import functools
import math

import jax
import jax.numpy as jnp
import numpy as np
from jax import lax
from jax.experimental import pallas as pl
from jax.experimental.pallas import tpu as pltpu
from jax.sharding import PartitionSpec as P

STEPS = 20
SAG_FACTOR = 0.3
F32 = jnp.float32
BF16 = jnp.bfloat16
MESH = pl.DeviceIdType.MESH
SUBS = 10
BLOCKS = 10
NEAR = 12
EARLY = 24
FIRST = (0, 1, 14)
REST = (11, 13, 2, 3, 4, 5, 6, 7, 8, 9, 10, 12, 15, 16, 17, 18)


def split(x):
    high = x.astype(BF16)
    return high, (x - high.astype(F32)).astype(BF16)


def mm(a, b):
    return lax.dot_general(a, b, (((1,), (0,)), ((), ())), preferred_element_type=F32)


def columns(row, count):
    return jnp.broadcast_to(row, (128, count)).T


def window_kernel(
    lines,
    convs,
    ports,
    far,
    zc_ref,
    waves_ref,
    hist_out_ref,
    state_out_ref,
    port_ref,
    bus_ref,
    big,
    wj,
    wx,
    cap2,
    xs,
    current_ref,
    zin,
    cin,
    vbus,
    flat_ref,
    rh,
    rl,
    zs,
    zr,
    zf,
    rs,
    rr,
    cs,
    cr,
    zlocal,
    os,
    orr,
    fs,
    xf,
    xr,
    olocal,
    picked,
    landed,
    ps,
    pr,
    out_early,
    out_late,
    in_early,
    in_late,
    base_ref,
    ws,
    wr,
    held,
    hs,
):
    loads = [pltpu.make_async_copy(there, here, hs.at[i]) for i, (there, here) in enumerate(zip(far, held))]
    for i in FIRST + REST:
        loads[i].start()
    (
        partner_ref,
        delay_ref,
        trig_ref,
        count_ref,
        line_node_ref,
        conv_node_ref,
        port_node_ref,
        line_adm_ref,
        conv_rate_ref,
        conv_limit_ref,
        port_adm_ref,
        ginv_ref,
        gcap_ref,
        hist_ref,
        past_ref,
        state_ref,
        target_ref,
        pvolt_ref,
        port_bus_ref,
    ) = held
    nodes = ginv_ref.shape[0]
    probes = 128
    half = lines // 2
    rows = 256
    areas, group = cin.shape[0], cin.shape[1]
    pieces, depth, width = zin.shape[0], zin.shape[2], zin.shape[3]
    inner = 2 ** ((areas.bit_length() - 1) // 2)
    outer = areas // inner
    span_rows = bus_ref.shape[1] // outer
    chunk = span_rows // inner
    a = lax.axis_index("area")
    r = lax.axis_index("row")
    zi = lax.div(a, inner)
    xi = lax.rem(a, inner)

    def subnet(by):
        to = lax.rem(a * group + r + by + areas * group, areas * group)
        return (lax.div(to, group), lax.rem(to, group))

    barrier = pltpu.get_barrier_semaphore()
    for d in range(1, areas):
        pl.semaphore_signal(barrier, inc=1, device_id=(lax.rem(a + d, areas), r), device_id_type=MESH)
    for d in range(1, group):
        pl.semaphore_signal(barrier, inc=1, device_id=(a, lax.rem(r + d, group)), device_id_type=MESH)
    for by in (1, -1, 2, -2):
        pl.semaphore_signal(barrier, inc=1, device_id=subnet(by), device_id_type=MESH)

    hist_steps = past_ref.shape[0] // lines
    for i in FIRST:
        loads[i].wait()
    late = hist_steps - EARLY
    pieces_of = (((out_early, in_early), 0, EARLY), ((out_late, in_late), EARLY, late))
    near = []
    place = []
    seen = jnp.int32(0)
    for l in range(half):
        gap = partner_ref[l] - (a * group + r)
        near.append((gap == 1) | (gap == 1 - areas * group))
        place.append(jnp.where(near[l], seen, NEAR + l - seen))
        seen = seen + jnp.where(near[l], 1, 0)
    for l in range(lines):
        start = jnp.clip(hist_steps - delay_ref[l], 0, hist_steps - STEPS)
        base_ref[0, l] = jnp.clip(place[l % half], 0, half - 1)
        base_ref[1, l] = start
    for k in range(half):
        line = jnp.int32(0)
        for l in range(half):
            line = line + jnp.where(place[l] == k, l, 0)
        line = jnp.clip(line, 0, half - 1)
        for side in range(2):
            for piece, (kept, first, count) in enumerate(pieces_of):
                source = pl.ds(first * lines + side * half + line, count, stride=lines)
                kept[0][side, k * count : (k + 1) * count, :] = past_ref[source, :]
    pl.semaphore_wait(barrier, areas + group + 2)

    def send(src, dst, ssem, rsem, to):
        return pltpu.make_async_remote_copy(
            src_ref=src, dst_ref=dst, send_sem=ssem, recv_sem=rsem, device_id=to, device_id_type=MESH
        )

    def wave_send(piece):
        (out, into), _, count = pieces_of[piece]
        copies = []
        for side, way in enumerate((1, -1)):
            for reach, slots in ((1, pl.ds(0, NEAR * count)), (2, pl.ds(NEAR * count, (half - NEAR) * count))):
                sem = (piece, 2 * side + reach - 1)
                copy = send(
                    out.at[side, slots, :], into.at[side, slots, :], ws.at[sem], wr.at[sem], subnet(way * reach)
                )
                copy.start()
                copies.append(copy)
        return copies

    early_sends = wave_send(0)
    late_sends = wave_send(1)

    def mate(e):
        return zi * inner + lax.rem(xi + e, inner)

    def part_of(plane, p):
        return zc_ref.at[:, pl.ds(pl.multiple_of((plane * pieces + p) * width, 128), width)]

    z_sends = []
    own_z = []
    for p in range(pieces):
        copy = pltpu.make_async_copy(part_of(zi, p), zin.at[p, a], zlocal.at[p])
        copy.start()
        own_z.append(copy)
        for d in range(1, outer):
            plane = lax.rem(zi + d, outer)
            copy = send(part_of(plane, p), zin.at[p, a], zs.at[p, d], zr.at[p, a], (plane * inner + xi, r))
            copy.start()
            z_sends.append(copy)
        for e in range(1, inner):
            copy = send(part_of(zi, p), zin.at[p, a], zf.at[p, 0, e], zr.at[p, a], (mate(e), r))
            copy.start()
            z_sends.append(copy)

    def relay_z(p):
        for d in range(1, outer):
            owner = lax.rem(zi + outer - d, outer) * inner + xi
            block = zin.at[p, owner]
            send(block, block, zs.at[p, d], zr.at[p, owner], (owner, r)).wait_recv()
            for e in range(1, inner):
                copy = send(block, block, zf.at[p, d, e], zr.at[p, owner], (mate(e), r))
                copy.start()
                z_sends.append(copy)

    for i in REST:
        loads[i].wait()
    pad = probes - lines - convs - ports

    def stacked(line, conv, port, rest):
        return jnp.concatenate(
            [columns(line, lines), columns(conv, convs), columns(port, ports), jnp.full((pad, 128), rest, F32)], axis=0
        )

    index = stacked(
        line_node_ref[...].astype(F32), conv_node_ref[...].astype(F32), port_node_ref[...].astype(F32), -1.0
    ).astype(jnp.int32)
    for c in range(nodes // 128):
        lane = lax.broadcasted_iota(jnp.int32, (probes, 128), 1) + 128 * c
        cap2[:, c * 128 : (c + 1) * 128] = jnp.where(index == lane, 1.0, 0.0)
    pick = cap2[...].astype(BF16)
    scatter = cap2[...].T.astype(BF16)
    for b in range(nodes // rows):
        span = pl.ds(b * rows, rows)
        high, low = split(ginv_ref[span, :])
        big[span, 0:nodes] = high
        big[span, nodes : 2 * nodes] = low
    tail = pl.ds(nodes, probes)
    big[tail, :nodes] = mm(pick, big[0:nodes, 0:nodes]).astype(BF16)
    big[tail, nodes : 2 * nodes] = mm(pick, big[0:nodes, nodes : 2 * nodes]).astype(BF16)
    big[:, 2 * nodes : 2 * nodes + 128] = mm(big[:, 0:nodes], scatter).astype(BF16)
    big[:, 2 * nodes + 128 :] = mm(big[:, nodes : 2 * nodes], scatter).astype(BF16)
    gcap = 2.0 * columns(gcap_ref[...], nodes)

    def put_state(value):
        high, low = split(value)
        wj[:, 0:128] = high
        wj[:, 128:256] = low

    hist_out_ref[...] = hist_ref[...]
    put_state(hist_ref[...])
    state_out_ref[...] = state_ref[...]
    current_ref[...] = jnp.zeros_like(current_ref)
    two_adm = 2.0 * columns(line_adm_ref[...], lines)
    rate = columns(conv_rate_ref[...], convs)
    limit = columns(conv_limit_ref[...], convs)
    padm = columns(port_adm_ref[...], ports)
    live = lax.broadcasted_iota(jnp.int32, (convs, 128), 0) < count_ref[0]
    xs[lines + convs + ports :, :] = jnp.zeros((probes - lines - convs - ports, 128), F32)

    def advance(both, t, carry):
        cosine = trig_ref[0, t]
        sine = trig_ref[1, t]
        for l in range(lines):
            side = 1 if l < half else 0
            slot = base_ref[0, l]
            when = base_ref[1, l] + t
            row = in_early[side, pl.ds(slot * EARLY + jnp.minimum(when, EARLY - 1), 1), :]
            if both:
                other = in_late[side, pl.ds(slot * late + jnp.maximum(when - EARLY, 0), 1), :]
                row = jnp.where(when < EARLY, row, other)
            xs[l : l + 1, :] = row
        inward = xs[0:lines, :]
        axial = state_out_ref[0]
        normal = state_out_ref[1]
        source = padm * (pvolt_ref[0] * cosine - pvolt_ref[1] * sine)
        xs[lines : lines + convs, :] = jnp.where(live, axial * cosine - normal * sine, 0.0)
        xs[lines + convs : lines + convs + ports, :] = source
        high, low = split(xs[...])
        wx[0:128, 0:128] = high
        wx[128:256, 0:128] = high
        wx[0:128, 128:256] = low
        wx[128:256, 128:256] = low

        def apply(start, size):
            span = pl.ds(start, size)
            both = (
                mm(big[span, 0:nodes], wj[...])
                + mm(big[span, nodes : 2 * nodes], wj[...])
                + mm(big[span, 2 * nodes :], wx[...])
            )
            return both[:, 0:128] + both[:, 128:256]

        probe = apply(nodes, probes)
        volts = apply(0, nodes)
        waves_ref[t] = two_adm * probe[0:lines] - inward
        emf = probe[lines : lines + convs]
        flow = source - padm * probe[lines + convs : lines + convs + ports]
        current_ref[0] += flow * cosine
        current_ref[1] -= flow * sine
        new_axial = axial + rate * (target_ref[0] - axial) - SAG_FACTOR * emf * cosine
        new_normal = normal + rate * (target_ref[1] - normal) + SAG_FACTOR * emf * sine
        state_out_ref[0] = jnp.where(live, limit * jnp.tanh(new_axial / limit), axial)
        state_out_ref[1] = jnp.where(live, limit * jnp.tanh(new_normal / limit), normal)
        after = gcap * volts - hist_out_ref[...]
        hist_out_ref[...] = after
        put_state(after)
        return carry

    for copy in early_sends:
        copy.wait()
    at = EARLY - hist_steps + STEPS
    lax.fori_loop(0, at, functools.partial(advance, False), 0)
    for copy in late_sends:
        copy.wait()
    step = functools.partial(advance, True)
    stops = [STEPS * 9 // 10 - (pieces - 1 - p) * STEPS * 2 // 5 for p in range(pieces)]
    for p, stop in enumerate(stops):
        lax.fori_loop(at, stop, step, 0)
        relay_z(p)
        at = stop
    lax.fori_loop(at, STEPS, step, 0)
    cin[a, r] = current_ref[...] * (2.0 / STEPS)

    copies = []
    for d in range(1, group):
        block = cin.at[a, r]
        copy = send(block, block, rs.at[d], rr.at[d], (a, lax.rem(r + d, group)))
        copy.start()
        copies.append(copy)
    for copy in copies:
        copy.wait()
    copies = []
    for d in range(1, areas):
        block = cin.at[a]
        copy = send(block, block, cs.at[d], cr.at[d], (lax.rem(a + d, areas), r))
        copy.start()
        copies.append(copy)
    for copy in copies:
        copy.wait()
    members = group * ports
    for i in range(areas):
        for j in range(group):
            re, im = cin[i, j, 0], cin[i, j, 1]
            top = i * depth + j * ports
            flat_ref[top : top + ports, 0:128] = re
            flat_ref[top : top + ports, 128:256] = im
            flat_ref[top + members : top + members + ports, 0:128] = -im
            flat_ref[top + members : top + members + ports, 128:256] = re
    high, low = split(flat_ref[...])
    rh[...] = high
    rl[...] = low

    for p in range(pieces):
        own_z[p].wait()
    for copy in z_sends:
        copy.wait_send()
    for p in range(pieces):
        for e in range(1, inner):
            for q in range(outer):
                owner = q * inner + lax.rem(xi + e, inner)
                block = zin.at[p, owner]
                send(block, block, zf.at[p, 0, e], zr.at[p, owner], (owner, r)).wait_recv()

    def product(p):
        high, low = split(zin[p].reshape(areas * depth, width).T)
        total = mm(high, rh[...]) + mm(low, rh[...]) + mm(high, rl[...])
        keep = min(width, span_rows)
        rows = pl.ds(pl.multiple_of(zi * span_rows + p * width, 8), keep)
        vbus[0, rows, :] = total[:keep, 0:128]
        vbus[1, rows, :] = total[:keep, 128:256]

    cuts = SUBS
    sub = chunk // cuts

    def region(plane, x, k):
        top = pl.multiple_of(plane * span_rows + x * chunk + k * sub, 8)
        return vbus.at[:, pl.ds(top, sub), :]

    def emit(plane, x, count, sem):
        rows = pl.ds(pl.multiple_of(plane * span_rows + x * chunk, 8), count)
        return pltpu.make_async_copy(vbus.at[:, rows, :], bus_ref.at[:, rows, :], sem)

    def plane_at(plane):
        return (plane * inner + xi, r)

    can_up = zi + 1 < outer
    can_down = zi >= 1

    def launch(k):
        up = send(region(zi, xi, k), region(zi, xi, k), os.at[0, k], orr.at[zi, k], plane_at(zi + 1))
        down = send(region(zi, xi, k), region(zi, xi, k), os.at[1, k], orr.at[zi, k], plane_at(zi - 1))
        return up, down

    if pieces == inner:
        product(xi)
    else:
        for p in range(pieces):
            product(p)
    for k in range(cuts):
        up, down = launch(k)
        pl.when(can_up)(up.start)
        pl.when(can_down)(down.start)
    if pieces == inner:
        for i in range(1, pieces):
            product(lax.rem(xi + i, inner))
    local = emit(zi, 0, span_rows, olocal.at[0, 0, 0])
    local.start()

    def hops(d):
        return ((zi - d, zi - d >= 0, zi + 1, can_up), (zi + d, zi + d < outer, zi - 1, can_down))

    def relay(plane, k, d, side, ahead):
        block = region(plane, xi, k)
        onward = send(block, block, fs.at[side, d, k], orr.at[plane, k], plane_at(ahead))
        across = [
            send(block, block, xf.at[side, d, e, k], xr.at[plane, xi, k], (mate(e), r)) for e in range(1, inner)
        ]
        return onward, across

    for d in range(1, outer):
        for k in range(cuts):
            for side, (plane, have, ahead, go) in enumerate(hops(d)):

                @pl.when(have)
                def _(plane=plane, k=k, d=d, side=side, ahead=ahead, go=go):
                    onward, across = relay(plane, k, d, side, ahead)
                    onward.wait_recv()
                    pl.when(go)(onward.start)
                    for copy in across:
                        copy.start()

    for d in range(1, outer):
        for side, (plane, have, ahead, go) in enumerate(hops(d)):

            @pl.when(have)
            def _(plane=plane, d=d, side=side):
                emit(plane, xi, chunk, olocal.at[side, d, 0]).start()
                for e in range(1, inner):
                    x = lax.rem(xi + e, inner)
                    for k in range(cuts):
                        block = region(plane, x, k)
                        send(block, block, xf.at[side, d, e, k], xr.at[plane, x, k], (mate(e), r)).wait_recv()
                    emit(plane, x, chunk, olocal.at[side, d, e]).start()

    members = port_bus_ref.shape[1]
    for j in range(group):
        for p in range(members):
            place = port_bus_ref[j, p] - r * bus_ref.shape[1]
            inside = (place >= 0) & (place < bus_ref.shape[1])
            place = jnp.clip(place, 0, bus_ref.shape[1] - 1)
            for part in range(2):
                value = vbus[part, pl.ds(place, 1), :]
                picked[j, part, p : p + 1, :] = jnp.where(inside, value, 0.0)

    def hand(d):
        to = lax.rem(r + d, group)
        return send(picked.at[to], landed.at[r], ps.at[d], pr.at[d], (a, to))

    for d in range(1, group):
        hand(d).start()
    for d in range(1, outer):
        for side, (plane, have, ahead, go) in enumerate(hops(d)):

            @pl.when(have)
            def _(plane=plane, d=d, side=side, ahead=ahead, go=go):
                for k in range(cuts):
                    onward, across = relay(plane, k, d, side, ahead)
                    pl.when(go)(onward.wait_send)
                    for copy in across:
                        copy.wait_send()
                for e in range(inner):
                    emit(plane, lax.rem(xi + e, inner), chunk, olocal.at[side, d, e]).wait()

    for k in range(cuts):
        up, down = launch(k)
        pl.when(can_up)(up.wait_send)
        pl.when(can_down)(down.wait_send)
    for d in range(1, group):
        hand(d).wait()
    value = picked[r]
    for d in range(1, group):
        value = value + landed[lax.rem(r + d, group)]
    port_ref[...] = value
    local.wait()


def vmem():
    return pl.BlockSpec(memory_space=pltpu.VMEM)


def emit_kernel(count, *refs):
    sources, targets = refs[:count], refs[count : 2 * count]
    held, sems, out_sems = refs[2 * count : 3 * count], refs[3 * count], refs[3 * count + 1]
    loads, stores = [], []
    for i in range(count):
        extent = sources[i].shape[0]
        cuts = BLOCKS if i == count - 1 else 1
        for k in range(cuts):
            rows = pl.ds(k * (extent // cuts), extent // cuts)
            slot = i + k
            loads.append(pltpu.make_async_copy(sources[i].at[rows], held[i].at[rows], sems.at[slot]))
            stores.append(pltpu.make_async_copy(held[i].at[rows], targets[i].at[rows], out_sems.at[slot]))
    order = list(range(count - 1, len(loads))) + list(range(count - 1))
    for n in order:
        loads[n].start()
    for n in order:
        loads[n].wait()
        stores[n].start()
    for n in order:
        stores[n].wait()


def emit_all(*arrays):
    flat = [x.reshape(-1, x.shape[-1]) for x in arrays]
    count = len(flat)
    slots = count - 1 + BLOCKS
    shapes = [jax.ShapeDtypeStruct(x.shape, x.dtype) for x in flat]
    done = pl.pallas_call(
        functools.partial(emit_kernel, count),
        out_shape=tuple(shapes),
        in_specs=[pl.BlockSpec(memory_space=pl.ANY)] * count,
        out_specs=(pl.BlockSpec(memory_space=pl.ANY),) * count,
        scratch_shapes=[pltpu.VMEM(x.shape, x.dtype) for x in flat]
        + [pltpu.SemaphoreType.DMA((slots,)), pltpu.SemaphoreType.DMA((slots,))],
        name="emit",
    )(*flat)
    return [y.reshape(x.shape) for x, y in zip(arrays, done)]


def hbm():
    return pl.BlockSpec(memory_space=pltpu.HBM)


def per_device(
    conductance_inverse,
    cap_history,
    cap_conductance,
    wave_history,
    line_partner,
    line_node,
    line_delay,
    line_admittance,
    conv_node,
    conv_count,
    conv_state,
    conv_reference,
    conv_rate,
    conv_limit,
    port_node,
    port_admittance,
    port_voltage_prev,
    port_bus,
    transfer_impedance,
):
    steps_kept, lines, cases = wave_history.shape[1:]
    nodes = conductance_inverse.shape[1]
    convs = conv_node.shape[1]
    ports = port_node.shape[1]
    areas = lax.axis_size("area")
    group = lax.axis_size("row")
    bus_rows = transfer_impedance.shape[1]
    members = transfer_impedance.shape[2]
    inner = 2 ** ((areas.bit_length() - 1) // 2)
    outer = areas // inner
    span_rows = bus_rows // outer
    padded = -(-span_rows // 128) * 128
    pieces = 2 if padded % 256 == 0 else 1
    zc = jnp.transpose(transfer_impedance, (0, 2, 1)).reshape(2 * members, outer, span_rows)
    zc = jnp.pad(zc, ((0, 0), (0, 0), (0, padded - span_rows))).reshape(2 * members, outer * padded)

    angles = np.arange(1, STEPS + 1, dtype=np.float32) * np.float32(2.0 * math.pi / STEPS)
    trig = jnp.asarray(np.stack([np.cos(angles), np.sin(angles)]).astype(np.float32))
    flops = 2 * STEPS * (nodes + 128) * (2 * nodes + 256) * 256
    inputs = [
        line_partner[0],
        line_delay[0],
        trig,
        conv_count,
        line_node,
        conv_node,
        port_node,
        line_admittance,
        conv_rate,
        conv_limit,
        port_admittance,
        conductance_inverse[0],
        cap_conductance,
        cap_history[0],
        wave_history.reshape(steps_kept * lines, cases),
        conv_state[0],
        conv_reference[0],
        port_voltage_prev[:, 0],
        port_bus,
    ]
    scalars = (0, 1, 2, 3, len(inputs) - 1)
    held = [
        (pltpu.SMEM if i in scalars else pltpu.VMEM)(x.shape, x.dtype) for i, x in enumerate(inputs)
    ]
    waves, hist_end, conv_out, port_voltage, bus_voltage = pl.pallas_call(
        functools.partial(window_kernel, lines, convs, ports),
        out_shape=(
            jax.ShapeDtypeStruct((STEPS, lines, cases), F32),
            jax.ShapeDtypeStruct((nodes, cases), F32),
            jax.ShapeDtypeStruct((2, convs, cases), F32),
            jax.ShapeDtypeStruct((2, ports, cases), F32),
            jax.ShapeDtypeStruct((2, bus_rows, cases), F32),
        ),
        in_specs=[[hbm()] * len(inputs), hbm()],
        out_specs=(vmem(),) * 4 + (pl.BlockSpec(memory_space=pl.ANY),),
        scratch_shapes=[
            pltpu.VMEM((nodes + 128, 2 * nodes + 256), BF16),
            pltpu.VMEM((nodes, 256), BF16),
            pltpu.VMEM((256, 256), BF16),
            pltpu.VMEM((128, nodes), F32),
            pltpu.VMEM((128, 128), F32),
            pltpu.VMEM((2, ports, cases), F32),
            pltpu.VMEM((pieces, areas, 2 * members, padded // pieces), F32),
            pltpu.VMEM((areas, group, 2, ports, cases), F32),
            pltpu.VMEM((2, bus_rows, cases), F32),
            pltpu.VMEM((areas * 2 * members, 2 * cases), F32),
            pltpu.VMEM((areas * 2 * members, 2 * cases), BF16),
            pltpu.VMEM((areas * 2 * members, 2 * cases), BF16),
            pltpu.SemaphoreType.DMA((pieces, outer)),
            pltpu.SemaphoreType.DMA((pieces, areas)),
            pltpu.SemaphoreType.DMA((pieces, outer, inner)),
            pltpu.SemaphoreType.DMA((group,)),
            pltpu.SemaphoreType.DMA((group,)),
            pltpu.SemaphoreType.DMA((areas,)),
            pltpu.SemaphoreType.DMA((areas,)),
            pltpu.SemaphoreType.DMA((pieces,)),
            pltpu.SemaphoreType.DMA((2, SUBS)),
            pltpu.SemaphoreType.DMA((outer, SUBS)),
            pltpu.SemaphoreType.DMA((2, outer, SUBS)),
            pltpu.SemaphoreType.DMA((2, outer, inner, SUBS)),
            pltpu.SemaphoreType.DMA((outer, inner, SUBS)),
            pltpu.SemaphoreType.DMA((2, outer, inner)),
            pltpu.VMEM((group, 2, ports, cases), F32),
            pltpu.VMEM((group, 2, ports, cases), F32),
            pltpu.SemaphoreType.DMA((group,)),
            pltpu.SemaphoreType.DMA((group,)),
            pltpu.VMEM((2, lines // 2 * EARLY, cases), F32),
            pltpu.VMEM((2, lines // 2 * (steps_kept - EARLY), cases), F32),
            pltpu.VMEM((2, lines // 2 * EARLY, cases), F32),
            pltpu.VMEM((2, lines // 2 * (steps_kept - EARLY), cases), F32),
            pltpu.SMEM((2, lines), jnp.int32),
            pltpu.SemaphoreType.DMA((2, 4)),
            pltpu.SemaphoreType.DMA((2, 4)),
            held,
            pltpu.SemaphoreType.DMA((len(inputs),)),
        ],
        compiler_params=pltpu.CompilerParams(collective_id=0, has_side_effects=True),
        cost_estimate=pl.CostEstimate(flops=flops, bytes_accessed=8_000_000, transcendentals=0),
        name="window",
    )(
        inputs,
        zc,
    )

    waves, hist_end, conv_out, port_voltage, bus_voltage = emit_all(waves, hist_end, conv_out, port_voltage, bus_voltage)
    return (waves[None], hist_end[None], conv_out[None], bus_voltage, port_voltage[:, None])


def solution(mesh):
    both = ("area", "row")
    placed = (
        P(both, None, None),
        P(both, None, None),
        P(both, None),
        P(both, None, None, None),
        P(both, None),
        P(both, None),
        P(both, None),
        P(both, None),
        P(both, None),
        P(both),
        P(both, None, None, None),
        P(both, None, None, None),
        P(both, None),
        P(both, None),
        P(both, None),
        P(both, None),
        P(None, both, None, None),
        P("area", None),
        P(None, "row", "area"),
    )
    return jax.shard_map(
        per_device,
        mesh=mesh,
        in_specs=placed,
        out_specs=(
            P(both, None, None, None),
            P(both, None, None),
            P(both, None, None, None),
            P(None, "row", None),
            P(None, both, None, None),
        ),
        check_vma=False,
    )
```

```python
import functools
import math

import jax
import jax.numpy as jnp
import numpy as np
from jax import lax
from jax.experimental import pallas as pl
from jax.experimental.pallas import tpu as pltpu
from jax.sharding import PartitionSpec as P

STEPS = 20
SAG_FACTOR = 0.3
F32 = jnp.float32
BF16 = jnp.bfloat16
MESH = pl.DeviceIdType.MESH
SUBS = 10
BLOCKS = 10
NEAR = 12
EARLY = 24
FIRST = (0, 1, 14)
REST = (11, 13, 2, 3, 4, 5, 6, 7, 8, 9, 10, 12, 15, 16, 17, 18)


def split(x):
    high = x.astype(BF16)
    return high, (x - high.astype(F32)).astype(BF16)


def mm(a, b):
    return lax.dot_general(a, b, (((1,), (0,)), ((), ())), preferred_element_type=F32)


def columns(row, count):
    return jnp.broadcast_to(row, (128, count)).T


def window_kernel(
    lines,
    convs,
    ports,
    far,
    zc_ref,
    waves_ref,
    hist_out_ref,
    state_out_ref,
    port_ref,
    bus_ref,
    big,
    wj,
    wx,
    cap2,
    xs,
    current_ref,
    zin,
    cin,
    vbus,
    flat_ref,
    rh,
    rl,
    zs,
    zr,
    zf,
    rs,
    rr,
    cs,
    cr,
    zlocal,
    os,
    orr,
    fs,
    xf,
    xr,
    olocal,
    picked,
    landed,
    ps,
    pr,
    out_early,
    out_late,
    in_early,
    in_late,
    base_ref,
    ws,
    wr,
    held,
    hs,
):
    loads = [pltpu.make_async_copy(there, here, hs.at[i]) for i, (there, here) in enumerate(zip(far, held))]
    for i in FIRST + REST:
        loads[i].start()
    (
        partner_ref,
        delay_ref,
        trig_ref,
        count_ref,
        line_node_ref,
        conv_node_ref,
        port_node_ref,
        line_adm_ref,
        conv_rate_ref,
        conv_limit_ref,
        port_adm_ref,
        ginv_ref,
        gcap_ref,
        hist_ref,
        past_ref,
        state_ref,
        target_ref,
        pvolt_ref,
        port_bus_ref,
    ) = held
    nodes = ginv_ref.shape[0]
    probes = 128
    half = lines // 2
    rows = 256
    areas, group = cin.shape[0], cin.shape[1]
    pieces, depth, width = zin.shape[0], zin.shape[2], zin.shape[3]
    inner = 2 ** ((areas.bit_length() - 1) // 2)
    outer = areas // inner
    span_rows = bus_ref.shape[1] // outer
    chunk = span_rows // inner
    a = lax.axis_index("area")
    r = lax.axis_index("row")
    zi = lax.div(a, inner)
    xi = lax.rem(a, inner)

    def subnet(by):
        to = lax.rem(a * group + r + by + areas * group, areas * group)
        return (lax.div(to, group), lax.rem(to, group))

    barrier = pltpu.get_barrier_semaphore()
    for d in range(1, areas):
        pl.semaphore_signal(barrier, inc=1, device_id=(lax.rem(a + d, areas), r), device_id_type=MESH)
    for d in range(1, group):
        pl.semaphore_signal(barrier, inc=1, device_id=(a, lax.rem(r + d, group)), device_id_type=MESH)
    for by in (1, -1, 2, -2):
        pl.semaphore_signal(barrier, inc=1, device_id=subnet(by), device_id_type=MESH)

    hist_steps = past_ref.shape[0] // lines
    for i in FIRST:
        loads[i].wait()
    late = hist_steps - EARLY
    pieces_of = (((out_early, in_early), 0, EARLY), ((out_late, in_late), EARLY, late))
    near = []
    place = []
    seen = jnp.int32(0)
    for l in range(half):
        gap = partner_ref[l] - (a * group + r)
        near.append((gap == 1) | (gap == 1 - areas * group))
        place.append(jnp.where(near[l], seen, NEAR + l - seen))
        seen = seen + jnp.where(near[l], 1, 0)
    for l in range(lines):
        start = jnp.clip(hist_steps - delay_ref[l], 0, hist_steps - STEPS)
        base_ref[0, l] = jnp.clip(place[l % half], 0, half - 1)
        base_ref[1, l] = start
    for k in range(half):
        line = jnp.int32(0)
        for l in range(half):
            line = line + jnp.where(place[l] == k, l, 0)
        line = jnp.clip(line, 0, half - 1)
        for side in range(2):
            for piece, (kept, first, count) in enumerate(pieces_of):
                source = pl.ds(first * lines + side * half + line, count, stride=lines)
                kept[0][side, k * count : (k + 1) * count, :] = past_ref[source, :]
    pl.semaphore_wait(barrier, areas + group + 2)

    def send(src, dst, ssem, rsem, to):
        return pltpu.make_async_remote_copy(
            src_ref=src, dst_ref=dst, send_sem=ssem, recv_sem=rsem, device_id=to, device_id_type=MESH
        )

    def wave_send(piece):
        (out, into), _, count = pieces_of[piece]
        copies = []
        for side, way in enumerate((1, -1)):
            for reach, slots in ((1, pl.ds(0, NEAR * count)), (2, pl.ds(NEAR * count, (half - NEAR) * count))):
                sem = (piece, 2 * side + reach - 1)
                copy = send(
                    out.at[side, slots, :], into.at[side, slots, :], ws.at[sem], wr.at[sem], subnet(way * reach)
                )
                copy.start()
                copies.append(copy)
        return copies

    early_sends = wave_send(0)
    late_sends = wave_send(1)

    def mate(e):
        return zi * inner + lax.rem(xi + e, inner)

    def part_of(plane, p):
        return zc_ref.at[:, pl.ds(pl.multiple_of((plane * pieces + p) * width, 128), width)]

    z_sends = []
    own_z = []
    for p in range(pieces):
        copy = pltpu.make_async_copy(part_of(zi, p), zin.at[p, a], zlocal.at[p])
        copy.start()
        own_z.append(copy)
        for d in range(1, outer):
            plane = lax.rem(zi + d, outer)
            copy = send(part_of(plane, p), zin.at[p, a], zs.at[p, d], zr.at[p, a], (plane * inner + xi, r))
            copy.start()
            z_sends.append(copy)
        for e in range(1, inner):
            copy = send(part_of(zi, p), zin.at[p, a], zf.at[p, 0, e], zr.at[p, a], (mate(e), r))
            copy.start()
            z_sends.append(copy)

    def relay_z(p):
        for d in range(1, outer):
            owner = lax.rem(zi + outer - d, outer) * inner + xi
            block = zin.at[p, owner]
            send(block, block, zs.at[p, d], zr.at[p, owner], (owner, r)).wait_recv()
            for e in range(1, inner):
                copy = send(block, block, zf.at[p, d, e], zr.at[p, owner], (mate(e), r))
                copy.start()
                z_sends.append(copy)

    for i in REST:
        loads[i].wait()
    pad = probes - lines - convs - ports

    def stacked(line, conv, port, rest):
        return jnp.concatenate(
            [columns(line, lines), columns(conv, convs), columns(port, ports), jnp.full((pad, 128), rest, F32)], axis=0
        )

    index = stacked(
        line_node_ref[...].astype(F32), conv_node_ref[...].astype(F32), port_node_ref[...].astype(F32), -1.0
    ).astype(jnp.int32)
    for c in range(nodes // 128):
        lane = lax.broadcasted_iota(jnp.int32, (probes, 128), 1) + 128 * c
        cap2[:, c * 128 : (c + 1) * 128] = jnp.where(index == lane, 1.0, 0.0)
    pick = cap2[...].astype(BF16)
    scatter = cap2[...].T.astype(BF16)
    for b in range(nodes // rows):
        span = pl.ds(b * rows, rows)
        high, low = split(ginv_ref[span, :])
        big[span, 0:nodes] = high
        big[span, nodes : 2 * nodes] = low
    tail = pl.ds(nodes, probes)
    big[tail, :nodes] = mm(pick, big[0:nodes, 0:nodes]).astype(BF16)
    big[tail, nodes : 2 * nodes] = mm(pick, big[0:nodes, nodes : 2 * nodes]).astype(BF16)
    big[:, 2 * nodes : 2 * nodes + 128] = mm(big[:, 0:nodes], scatter).astype(BF16)
    big[:, 2 * nodes + 128 :] = mm(big[:, nodes : 2 * nodes], scatter).astype(BF16)
    gcap = 2.0 * columns(gcap_ref[...], nodes)

    def put_state(value):
        high, low = split(value)
        wj[:, 0:128] = high
        wj[:, 128:256] = low

    hist_out_ref[...] = hist_ref[...]
    put_state(hist_ref[...])
    state_out_ref[...] = state_ref[...]
    current_ref[...] = jnp.zeros_like(current_ref)
    two_adm = 2.0 * columns(line_adm_ref[...], lines)
    rate = columns(conv_rate_ref[...], convs)
    limit = columns(conv_limit_ref[...], convs)
    padm = columns(port_adm_ref[...], ports)
    live = lax.broadcasted_iota(jnp.int32, (convs, 128), 0) < count_ref[0]
    xs[lines + convs + ports :, :] = jnp.zeros((probes - lines - convs - ports, 128), F32)

    def advance(both, t, carry):
        cosine = trig_ref[0, t]
        sine = trig_ref[1, t]
        for l in range(lines):
            side = 1 if l < half else 0
            slot = base_ref[0, l]
            when = base_ref[1, l] + t
            row = in_early[side, pl.ds(slot * EARLY + jnp.minimum(when, EARLY - 1), 1), :]
            if both:
                other = in_late[side, pl.ds(slot * late + jnp.maximum(when - EARLY, 0), 1), :]
                row = jnp.where(when < EARLY, row, other)
            xs[l : l + 1, :] = row
        inward = xs[0:lines, :]
        axial = state_out_ref[0]
        normal = state_out_ref[1]
        source = padm * (pvolt_ref[0] * cosine - pvolt_ref[1] * sine)
        xs[lines : lines + convs, :] = jnp.where(live, axial * cosine - normal * sine, 0.0)
        xs[lines + convs : lines + convs + ports, :] = source
        high, low = split(xs[...])
        wx[0:128, 0:128] = high
        wx[128:256, 0:128] = high
        wx[0:128, 128:256] = low
        wx[128:256, 128:256] = low

        def apply(start, size):
            span = pl.ds(start, size)
            both = (
                mm(big[span, 0:nodes], wj[...])
                + mm(big[span, nodes : 2 * nodes], wj[...])
                + mm(big[span, 2 * nodes :], wx[...])
            )
            return both[:, 0:128] + both[:, 128:256]

        probe = apply(nodes, probes)
        volts = apply(0, nodes)
        waves_ref[t] = two_adm * probe[0:lines] - inward
        emf = probe[lines : lines + convs]
        flow = source - padm * probe[lines + convs : lines + convs + ports]
        current_ref[0] += flow * cosine
        current_ref[1] -= flow * sine
        new_axial = axial + rate * (target_ref[0] - axial) - SAG_FACTOR * emf * cosine
        new_normal = normal + rate * (target_ref[1] - normal) + SAG_FACTOR * emf * sine
        state_out_ref[0] = jnp.where(live, limit * jnp.tanh(new_axial / limit), axial)
        state_out_ref[1] = jnp.where(live, limit * jnp.tanh(new_normal / limit), normal)
        after = gcap * volts - hist_out_ref[...]
        hist_out_ref[...] = after
        put_state(after)
        return carry

    for copy in early_sends:
        copy.wait()
    at = EARLY - hist_steps + STEPS
    lax.fori_loop(0, at, functools.partial(advance, False), 0)
    for copy in late_sends:
        copy.wait()
    step = functools.partial(advance, True)
    stops = [STEPS * 9 // 10 - (pieces - 1 - p) * STEPS * 2 // 5 for p in range(pieces)]
    for p, stop in enumerate(stops):
        lax.fori_loop(at, stop, step, 0)
        relay_z(p)
        at = stop
    lax.fori_loop(at, STEPS, step, 0)
    cin[a, r] = current_ref[...] * (2.0 / STEPS)

    copies = []
    for d in range(1, group):
        block = cin.at[a, r]
        copy = send(block, block, rs.at[d], rr.at[d], (a, lax.rem(r + d, group)))
        copy.start()
        copies.append(copy)
    for copy in copies:
        copy.wait()
    copies = []
    for d in range(1, areas):
        block = cin.at[a]
        copy = send(block, block, cs.at[d], cr.at[d], (lax.rem(a + d, areas), r))
        copy.start()
        copies.append(copy)
    for copy in copies:
        copy.wait()
    members = group * ports
    for i in range(areas):
        for j in range(group):
            re, im = cin[i, j, 0], cin[i, j, 1]
            top = i * depth + j * ports
            flat_ref[top : top + ports, 0:128] = re
            flat_ref[top : top + ports, 128:256] = im
            flat_ref[top + members : top + members + ports, 0:128] = -im
            flat_ref[top + members : top + members + ports, 128:256] = re
    high, low = split(flat_ref[...])
    rh[...] = high
    rl[...] = low

    for p in range(pieces):
        own_z[p].wait()
    for p in range(pieces):
        for e in range(1, inner):
            for q in range(outer):
                owner = q * inner + lax.rem(xi + e, inner)
                block = zin.at[p, owner]
                send(block, block, zf.at[p, 0, e], zr.at[p, owner], (owner, r)).wait_recv()

    def product(p):
        high, low = split(zin[p].reshape(areas * depth, width).T)
        total = mm(high, rh[...]) + mm(low, rh[...]) + mm(high, rl[...])
        keep = min(width, span_rows)
        rows = pl.ds(pl.multiple_of(zi * span_rows + p * width, 8), keep)
        vbus[0, rows, :] = total[:keep, 0:128]
        vbus[1, rows, :] = total[:keep, 128:256]

    cuts = SUBS
    sub = chunk // cuts

    def region(plane, x, k):
        top = pl.multiple_of(plane * span_rows + x * chunk + k * sub, 8)
        return vbus.at[:, pl.ds(top, sub), :]

    def emit(plane, x, count, sem):
        rows = pl.ds(pl.multiple_of(plane * span_rows + x * chunk, 8), count)
        return pltpu.make_async_copy(vbus.at[:, rows, :], bus_ref.at[:, rows, :], sem)

    def plane_at(plane):
        return (plane * inner + xi, r)

    can_up = zi + 1 < outer
    can_down = zi >= 1

    def launch(k):
        up = send(region(zi, xi, k), region(zi, xi, k), os.at[0, k], orr.at[zi, k], plane_at(zi + 1))
        down = send(region(zi, xi, k), region(zi, xi, k), os.at[1, k], orr.at[zi, k], plane_at(zi - 1))
        return up, down

    if pieces == inner:
        product(xi)
    else:
        for p in range(pieces):
            product(p)
    for k in range(cuts):
        up, down = launch(k)
        pl.when(can_up)(up.start)
        pl.when(can_down)(down.start)
    if pieces == inner:
        for i in range(1, pieces):
            product(lax.rem(xi + i, inner))
    local = emit(zi, 0, span_rows, olocal.at[0, 0, 0])
    local.start()

    def hops(d):
        return ((zi - d, zi - d >= 0, zi + 1, can_up), (zi + d, zi + d < outer, zi - 1, can_down))

    def relay(plane, k, d, side, ahead):
        block = region(plane, xi, k)
        onward = send(block, block, fs.at[side, d, k], orr.at[plane, k], plane_at(ahead))
        across = [
            send(block, block, xf.at[side, d, e, k], xr.at[plane, xi, k], (mate(e), r)) for e in range(1, inner)
        ]
        return onward, across

    for d in range(1, outer):
        for k in range(cuts):
            for side, (plane, have, ahead, go) in enumerate(hops(d)):

                @pl.when(have)
                def _(plane=plane, k=k, d=d, side=side, ahead=ahead, go=go):
                    onward, across = relay(plane, k, d, side, ahead)
                    onward.wait_recv()
                    pl.when(go)(onward.start)
                    for copy in across:
                        copy.start()

    for d in range(1, outer):
        for side, (plane, have, ahead, go) in enumerate(hops(d)):

            @pl.when(have)
            def _(plane=plane, d=d, side=side):
                emit(plane, xi, chunk, olocal.at[side, d, 0]).start()
                for e in range(1, inner):
                    x = lax.rem(xi + e, inner)
                    for k in range(cuts):
                        block = region(plane, x, k)
                        send(block, block, xf.at[side, d, e, k], xr.at[plane, x, k], (mate(e), r)).wait_recv()
                    emit(plane, x, chunk, olocal.at[side, d, e]).start()

    members = port_bus_ref.shape[1]
    for j in range(group):
        for p in range(members):
            place = port_bus_ref[j, p] - r * bus_ref.shape[1]
            inside = (place >= 0) & (place < bus_ref.shape[1])
            place = jnp.clip(place, 0, bus_ref.shape[1] - 1)
            for part in range(2):
                value = vbus[part, pl.ds(place, 1), :]
                picked[j, part, p : p + 1, :] = jnp.where(inside, value, 0.0)

    def hand(d):
        to = lax.rem(r + d, group)
        return send(picked.at[to], landed.at[r], ps.at[d], pr.at[d], (a, to))

    for d in range(1, group):
        hand(d).start()
    for d in range(1, outer):
        for side, (plane, have, ahead, go) in enumerate(hops(d)):

            @pl.when(have)
            def _(plane=plane, d=d, side=side, ahead=ahead, go=go):
                for k in range(cuts):
                    onward, across = relay(plane, k, d, side, ahead)
                    pl.when(go)(onward.wait_send)
                    for copy in across:
                        copy.wait_send()
                for e in range(inner):
                    emit(plane, lax.rem(xi + e, inner), chunk, olocal.at[side, d, e]).wait()

    for k in range(cuts):
        up, down = launch(k)
        pl.when(can_up)(up.wait_send)
        pl.when(can_down)(down.wait_send)
    for copy in z_sends:
        copy.wait_send()
    for d in range(1, group):
        hand(d).wait()
    value = picked[r]
    for d in range(1, group):
        value = value + landed[lax.rem(r + d, group)]
    port_ref[...] = value
    local.wait()


def vmem():
    return pl.BlockSpec(memory_space=pltpu.VMEM)


def emit_kernel(count, *refs):
    sources, targets = refs[:count], refs[count : 2 * count]
    held, sems, out_sems = refs[2 * count : 3 * count], refs[3 * count], refs[3 * count + 1]
    loads, stores = [], []
    for i in range(count):
        extent = sources[i].shape[0]
        cuts = BLOCKS if i == count - 1 else 1
        for k in range(cuts):
            rows = pl.ds(k * (extent // cuts), extent // cuts)
            slot = i + k
            loads.append(pltpu.make_async_copy(sources[i].at[rows], held[i].at[rows], sems.at[slot]))
            stores.append(pltpu.make_async_copy(held[i].at[rows], targets[i].at[rows], out_sems.at[slot]))
    order = list(range(count - 1, len(loads))) + list(range(count - 1))
    for n in order:
        loads[n].start()
    for n in order:
        loads[n].wait()
        stores[n].start()
    for n in order:
        stores[n].wait()


def emit_all(*arrays):
    flat = [x.reshape(-1, x.shape[-1]) for x in arrays]
    count = len(flat)
    slots = count - 1 + BLOCKS
    shapes = [jax.ShapeDtypeStruct(x.shape, x.dtype) for x in flat]
    done = pl.pallas_call(
        functools.partial(emit_kernel, count),
        out_shape=tuple(shapes),
        in_specs=[pl.BlockSpec(memory_space=pl.ANY)] * count,
        out_specs=(pl.BlockSpec(memory_space=pl.ANY),) * count,
        scratch_shapes=[pltpu.VMEM(x.shape, x.dtype) for x in flat]
        + [pltpu.SemaphoreType.DMA((slots,)), pltpu.SemaphoreType.DMA((slots,))],
        name="emit",
    )(*flat)
    return [y.reshape(x.shape) for x, y in zip(arrays, done)]


def hbm():
    return pl.BlockSpec(memory_space=pltpu.HBM)


def per_device(
    conductance_inverse,
    cap_history,
    cap_conductance,
    wave_history,
    line_partner,
    line_node,
    line_delay,
    line_admittance,
    conv_node,
    conv_count,
    conv_state,
    conv_reference,
    conv_rate,
    conv_limit,
    port_node,
    port_admittance,
    port_voltage_prev,
    port_bus,
    transfer_impedance,
):
    steps_kept, lines, cases = wave_history.shape[1:]
    nodes = conductance_inverse.shape[1]
    convs = conv_node.shape[1]
    ports = port_node.shape[1]
    areas = lax.axis_size("area")
    group = lax.axis_size("row")
    bus_rows = transfer_impedance.shape[1]
    members = transfer_impedance.shape[2]
    inner = 2 ** ((areas.bit_length() - 1) // 2)
    outer = areas // inner
    span_rows = bus_rows // outer
    padded = -(-span_rows // 128) * 128
    pieces = 2 if padded % 256 == 0 else 1
    zc = jnp.transpose(transfer_impedance, (0, 2, 1)).reshape(2 * members, outer, span_rows)
    zc = jnp.pad(zc, ((0, 0), (0, 0), (0, padded - span_rows))).reshape(2 * members, outer * padded)

    angles = np.arange(1, STEPS + 1, dtype=np.float32) * np.float32(2.0 * math.pi / STEPS)
    trig = jnp.asarray(np.stack([np.cos(angles), np.sin(angles)]).astype(np.float32))
    flops = 2 * STEPS * (nodes + 128) * (2 * nodes + 256) * 256
    inputs = [
        line_partner[0],
        line_delay[0],
        trig,
        conv_count,
        line_node,
        conv_node,
        port_node,
        line_admittance,
        conv_rate,
        conv_limit,
        port_admittance,
        conductance_inverse[0],
        cap_conductance,
        cap_history[0],
        wave_history.reshape(steps_kept * lines, cases),
        conv_state[0],
        conv_reference[0],
        port_voltage_prev[:, 0],
        port_bus,
    ]
    scalars = (0, 1, 2, 3, len(inputs) - 1)
    held = [
        (pltpu.SMEM if i in scalars else pltpu.VMEM)(x.shape, x.dtype) for i, x in enumerate(inputs)
    ]
    waves, hist_end, conv_out, port_voltage, bus_voltage = pl.pallas_call(
        functools.partial(window_kernel, lines, convs, ports),
        out_shape=(
            jax.ShapeDtypeStruct((STEPS, lines, cases), F32),
            jax.ShapeDtypeStruct((nodes, cases), F32),
            jax.ShapeDtypeStruct((2, convs, cases), F32),
            jax.ShapeDtypeStruct((2, ports, cases), F32),
            jax.ShapeDtypeStruct((2, bus_rows, cases), F32),
        ),
        in_specs=[[hbm()] * len(inputs), hbm()],
        out_specs=(vmem(),) * 4 + (pl.BlockSpec(memory_space=pl.ANY),),
        scratch_shapes=[
            pltpu.VMEM((nodes + 128, 2 * nodes + 256), BF16),
            pltpu.VMEM((nodes, 256), BF16),
            pltpu.VMEM((256, 256), BF16),
            pltpu.VMEM((128, nodes), F32),
            pltpu.VMEM((128, 128), F32),
            pltpu.VMEM((2, ports, cases), F32),
            pltpu.VMEM((pieces, areas, 2 * members, padded // pieces), F32),
            pltpu.VMEM((areas, group, 2, ports, cases), F32),
            pltpu.VMEM((2, bus_rows, cases), F32),
            pltpu.VMEM((areas * 2 * members, 2 * cases), F32),
            pltpu.VMEM((areas * 2 * members, 2 * cases), BF16),
            pltpu.VMEM((areas * 2 * members, 2 * cases), BF16),
            pltpu.SemaphoreType.DMA((pieces, outer)),
            pltpu.SemaphoreType.DMA((pieces, areas)),
            pltpu.SemaphoreType.DMA((pieces, outer, inner)),
            pltpu.SemaphoreType.DMA((group,)),
            pltpu.SemaphoreType.DMA((group,)),
            pltpu.SemaphoreType.DMA((areas,)),
            pltpu.SemaphoreType.DMA((areas,)),
            pltpu.SemaphoreType.DMA((pieces,)),
            pltpu.SemaphoreType.DMA((2, SUBS)),
            pltpu.SemaphoreType.DMA((outer, SUBS)),
            pltpu.SemaphoreType.DMA((2, outer, SUBS)),
            pltpu.SemaphoreType.DMA((2, outer, inner, SUBS)),
            pltpu.SemaphoreType.DMA((outer, inner, SUBS)),
            pltpu.SemaphoreType.DMA((2, outer, inner)),
            pltpu.VMEM((group, 2, ports, cases), F32),
            pltpu.VMEM((group, 2, ports, cases), F32),
            pltpu.SemaphoreType.DMA((group,)),
            pltpu.SemaphoreType.DMA((group,)),
            pltpu.VMEM((2, lines // 2 * EARLY, cases), F32),
            pltpu.VMEM((2, lines // 2 * (steps_kept - EARLY), cases), F32),
            pltpu.VMEM((2, lines // 2 * EARLY, cases), F32),
            pltpu.VMEM((2, lines // 2 * (steps_kept - EARLY), cases), F32),
            pltpu.SMEM((2, lines), jnp.int32),
            pltpu.SemaphoreType.DMA((2, 4)),
            pltpu.SemaphoreType.DMA((2, 4)),
            held,
            pltpu.SemaphoreType.DMA((len(inputs),)),
        ],
        compiler_params=pltpu.CompilerParams(collective_id=0, has_side_effects=True),
        cost_estimate=pl.CostEstimate(flops=flops, bytes_accessed=8_000_000, transcendentals=0),
        name="window",
    )(
        inputs,
        zc,
    )

    waves, hist_end, conv_out, port_voltage, bus_voltage = emit_all(waves, hist_end, conv_out, port_voltage, bus_voltage)
    return (waves[None], hist_end[None], conv_out[None], bus_voltage, port_voltage[:, None])


def solution(mesh):
    both = ("area", "row")
    placed = (
        P(both, None, None),
        P(both, None, None),
        P(both, None),
        P(both, None, None, None),
        P(both, None),
        P(both, None),
        P(both, None),
        P(both, None),
        P(both, None),
        P(both),
        P(both, None, None, None),
        P(both, None, None, None),
        P(both, None),
        P(both, None),
        P(both, None),
        P(both, None),
        P(None, both, None, None),
        P("area", None),
        P(None, "row", "area"),
    )
    return jax.shard_map(
        per_device,
        mesh=mesh,
        in_specs=placed,
        out_specs=(
            P(both, None, None, None),
            P(both, None, None),
            P(both, None, None, None),
            P(None, "row", None),
            P(None, both, None, None),
        ),
        check_vma=False,
    )
```
